32 devices in a mesh: dp: 4 (over x, core), seq: 8 (over z, y).
Axes of the slice: x: 2, y: 2, z: 4, core: 2. Of those that a mesh axis runs over, the one named last changes fastest.
Arguments:
- tokens: bfloat16 [4, 2048, 1024], P('dp', 'seq'), may hold values from -6 to 6
- cotangent: bfloat16 [4, 2048, 1024], P('dp', 'seq'), may hold values from -6 to 6
- first_factor: bfloat16 [8, 256, 256], P('seq'), may hold values from -0.375 to 0.375
- second_factor: bfloat16 [8, 256, 8], P(None, 'seq'), may hold values from -2 to 2
- norm_gain: float32 [1024], replicated, may hold values from 0.25 to 1.75
- gate_scale: float32 [1024], replicated, may hold values from -4 to 4
- gate_bias: float32 [1024], replicated, may hold values from -4 to 4
- mlp_gain: float32 [1024], replicated, may hold values from 0.25 to 1.75
- gate_weight: bfloat16 [8, 128, 512], replicated, may hold values from -0.5 to 0.5
- up_weight: bfloat16 [8, 128, 512], replicated, may hold values from -0.5 to 0.5
- down_weight: bfloat16 [8, 128, 512], replicated, may hold values from -0.25 to 0.25
Outputs:
- grad_tokens: bfloat16 [4, 2048, 1024], P('dp', 'seq')
- grad_first: float32 [8, 256, 256], P('seq', None, 'dp')
- grad_second: float32 [8, 256, 8], P(None, 'seq', 'dp')
- grad_gate: float32 [8, 128, 512], P('dp', None, 'seq')
- grad_up: float32 [8, 128, 512], P('dp', None, 'seq')
- grad_down: float32 [8, 128, 512], P('dp', None, 'seq')
The draws below stay inside these ranges and needn't reach their ends.
All inputs are finite; a program needn't handle non-finite values.
Results may differ from the reference program's by a relative error of at most 0.017.
Values may be sent and summed in bfloat16 or wider, within the bound.
A program may use at most 128 MiB of HBM per device.

```python
import jax
import jax.numpy as jnp
from jax import lax

D = 1024
MB = 8
BLK = 256
SEQS = 4
L = 2048
NB = 8
DB = 128
HB = 512


def block_levels(rng, extent, shards, least, largest):
    loudness = 1.0
    for dim, shards_of in shards:
        steps = jax.random.uniform(jax.random.fold_in(jax.random.fold_in(rng, 6), dim), (shards_of,), jnp.float32, least / len(shards), largest / len(shards))
        loudness = loudness * jnp.repeat(jnp.exp(steps), extent[dim] // shards_of).reshape((-1,) + (1,) * (len(extent) - 1 - dim))
    return loudness


def noise(rng, extent, deviation, bound, cuts=(), dtype=jnp.bfloat16):
    drawn = deviation * jax.random.normal(rng, extent, jnp.float32)
    if cuts:
        drawn = drawn * block_levels(rng, extent, cuts, -0.22, 0.18)
    return jnp.clip(drawn, -bound, bound).astype(dtype)


def setup_inputs(seed: int = 0) -> dict:
    seeds = jax.random.split(jax.random.key(seed), 12)
    return {
        "tokens": noise(seeds[0], (SEQS, L, D), 1.0, 6.0, ((0, 4), (1, 8))),
        "cotangent": noise(seeds[1], (SEQS, L, D), 1.0, 6.0, ((0, 4), (1, 8))),
        "first_factor": noise(seeds[2], (NB, BLK, BLK), BLK ** -0.5, 0.375, ((0, 8),)),
        "second_factor": noise(seeds[3], (NB, BLK, NB), NB ** -0.5, 2.0, ((1, 8),)),
        "norm_gain": jnp.clip(1.0 + 0.15 * jax.random.normal(seeds[4], (D,), jnp.float32), 0.25, 1.75),
        "gate_scale": noise(seeds[5], (D,), 1.0, 4.0, (), jnp.float32),
        "gate_bias": noise(seeds[6], (D,), 1.0, 4.0, (), jnp.float32),
        "mlp_gain": jnp.clip(1.0 + 0.15 * jax.random.normal(seeds[7], (D,), jnp.float32), 0.25, 1.75),
        "gate_weight": noise(seeds[8], (MB, DB, HB), DB ** -0.5, 0.5),
        "up_weight": noise(seeds[9], (MB, DB, HB), DB ** -0.5, 0.5),
        "down_weight": noise(seeds[10], (MB, DB, HB), HB ** -0.5, 0.25),
    }


epsilon = 1e-05

def inverse_rms(values):
    return lax.rsqrt(lax.optimization_barrier(jnp.mean(values * values, axis=-1, keepdims=True)) + epsilon)

def norm_backward(grad_normed, normed_values, inverse):
    return inverse * (grad_normed - normed_values * lax.optimization_barrier(jnp.mean(grad_normed * normed_values, axis=-1, keepdims=True)))

def wide_einsum(pattern, left_side, right_side):
    return jnp.einsum(pattern, left_side.astype(jnp.float32), right_side.astype(jnp.float32))

def one_sequence(inputs, upstream, first_factor, second_factor, norm_gain, gate_scale, gate_bias, mlp_gain, gate_weight, up_weight, down_weight):
    inputs_wide = inputs.astype(jnp.float32)
    first_inverse = inverse_rms(inputs_wide)
    first_normed = inputs_wide * first_inverse
    normed_tokens = (first_normed * norm_gain).astype(jnp.bfloat16)
    blocked = normed_tokens.reshape(NB, BLK, D)
    section_one = wide_einsum('bij,bjd->bid', first_factor, blocked).astype(jnp.bfloat16)
    mixed_seq = wide_einsum('cib,bid->cid', second_factor, section_one).astype(jnp.bfloat16).reshape(L, D)
    mixed_wide = mixed_seq.astype(jnp.float32)
    gate_open = jax.nn.sigmoid(normed_tokens.astype(jnp.float32) * gate_scale + gate_bias)
    after_mix = (inputs_wide + mixed_wide * gate_open).astype(jnp.bfloat16)
    after_wide = after_mix.astype(jnp.float32)
    second_inverse = inverse_rms(after_wide)
    second_normed = after_wide * second_inverse
    mlp_input = (second_normed * mlp_gain).astype(jnp.bfloat16).reshape(L, MB, DB)
    pre_gate = wide_einsum('tkd,kdh->tkh', mlp_input, gate_weight)
    pre_up = wide_einsum('tkd,kdh->tkh', mlp_input, up_weight)
    sig_gate = jax.nn.sigmoid(pre_gate)
    hidden = (pre_gate * sig_gate * pre_up).astype(jnp.bfloat16)
    permuted = jnp.transpose(hidden, (0, 2, 1)).reshape(L, MB, HB)
    upstream_wide = upstream.astype(jnp.float32)
    upstream_blocks = upstream.reshape(L, MB, DB)
    grad_perm = wide_einsum('tkd,kdh->tkh', upstream_blocks, down_weight).astype(jnp.bfloat16)
    down_term = wide_einsum('tkd,tkh->kdh', upstream_blocks, permuted)
    grad_hidden = jnp.transpose(grad_perm.reshape(L, HB, MB), (0, 2, 1)).astype(jnp.float32)
    grad_gate_pre = (grad_hidden * pre_up * sig_gate * (1.0 + pre_gate * (1.0 - sig_gate))).astype(jnp.bfloat16)
    grad_up_pre = (grad_hidden * pre_gate * sig_gate).astype(jnp.bfloat16)
    gate_term = wide_einsum('tkd,tkh->kdh', mlp_input, grad_gate_pre)
    up_term = wide_einsum('tkd,tkh->kdh', mlp_input, grad_up_pre)
    grad_inner = wide_einsum('tkh,kdh->tkd', grad_gate_pre, gate_weight) + wide_einsum('tkh,kdh->tkd', grad_up_pre, up_weight)
    grad_inner = grad_inner.reshape(L, D)
    grad_after = (upstream_wide + norm_backward(grad_inner * mlp_gain, second_normed, second_inverse)).astype(jnp.bfloat16)
    grad_after_wide = grad_after.astype(jnp.float32)
    grad_mixed = (grad_after_wide * gate_open).astype(jnp.bfloat16)
    grad_open = grad_after_wide * mixed_wide * gate_open * (1.0 - gate_open)
    grad_mixed_blocks = grad_mixed.reshape(NB, BLK, D)
    grad_section = wide_einsum('cib,cid->bid', second_factor, grad_mixed_blocks).astype(jnp.bfloat16)
    second_term = wide_einsum('cid,bid->cib', grad_mixed_blocks, section_one)
    first_term = wide_einsum('bid,bjd->bij', grad_section, blocked)
    grad_normed = wide_einsum('bij,bid->bjd', first_factor, grad_section).reshape(L, D) + grad_open * gate_scale
    grad_inputs = (grad_after_wide + norm_backward(grad_normed * norm_gain, first_normed, first_inverse)).astype(jnp.bfloat16)
    return (grad_inputs, first_term, second_term, gate_term, up_term, down_term)

def reference(tokens, cotangent, first_factor, second_factor, norm_gain, gate_scale, gate_bias, mlp_gain, gate_weight, up_weight, down_weight):
    grads_list = []
    first_total = jnp.zeros((NB, BLK, BLK), jnp.float32)
    second_total = jnp.zeros((NB, BLK, NB), jnp.float32)
    gate_total = jnp.zeros((MB, DB, HB), jnp.float32)
    up_total = jnp.zeros((MB, DB, HB), jnp.float32)
    down_total = jnp.zeros((MB, DB, HB), jnp.float32)
    for sequence in range(SEQS):
        outcome = one_sequence(tokens[sequence], cotangent[sequence], first_factor, second_factor, norm_gain, gate_scale, gate_bias, mlp_gain, gate_weight, up_weight, down_weight)
        grads_list.append(outcome[0])
        first_total = first_total + outcome[1]
        second_total = second_total + outcome[2]
        gate_total = gate_total + outcome[3]
        up_total = up_total + outcome[4]
        down_total = down_total + outcome[5]
    factor_weight = (SEQS * D) ** (-0.5)
    mlp_weight = (SEQS * L) ** (-0.5)
    return (jnp.stack(grads_list), first_total * factor_weight, second_total * factor_weight, gate_total * mlp_weight, up_total * mlp_weight, down_total * mlp_weight)
```

```python
import jax
import jax.numpy as jnp
from jax import lax
from jax.experimental import pallas as pl
from jax.experimental.pallas import tpu as pltpu
from jax.sharding import PartitionSpec as P

epsilon = 1e-05


def inverse_rms(values):
    return lax.rsqrt(jnp.mean(values * values, axis=-1, keepdims=True) + epsilon)


def norm_backward(grad_normed, normed_values, inverse):
    return inverse * (
        grad_normed - normed_values * jnp.mean(grad_normed * normed_values, axis=-1, keepdims=True)
    )


def plain_body(
    tokens,
    cotangent,
    first_factor,
    second_factor,
    norm_gain,
    gate_scale,
    gate_bias,
    mlp_gain,
    gate_weight,
    up_weight,
    down_weight,
):
    inputs = tokens[0]
    upstream = cotangent[0]
    rows_local, width = inputs.shape
    local_blocks, block_size = (first_factor.shape[0], first_factor.shape[1])
    mlp_blocks, block_in, block_hidden = gate_weight.shape
    inputs_wide = inputs.astype(jnp.float32)
    first_inverse = inverse_rms(inputs_wide)
    first_normed = inputs_wide * first_inverse
    normed_tokens = (first_normed * norm_gain).astype(jnp.bfloat16)
    blocked = normed_tokens.reshape(local_blocks, block_size, width)
    section_one = jnp.einsum(
        "bij,bjd->bid", first_factor, blocked, preferred_element_type=jnp.float32
    ).astype(jnp.bfloat16)
    section_cols = lax.all_to_all(section_one, "seq", split_axis=1, concat_axis=0, tiled=True)
    mixed_cols = jnp.einsum(
        "cib,bid->cid", second_factor, section_cols, preferred_element_type=jnp.float32
    ).astype(jnp.bfloat16)
    mixed_rows = lax.all_to_all(mixed_cols, "seq", split_axis=0, concat_axis=1, tiled=True).reshape(
        rows_local, width
    )
    mixed_wide = mixed_rows.astype(jnp.float32)
    gate_open = jax.nn.sigmoid(normed_tokens.astype(jnp.float32) * gate_scale + gate_bias)
    after_mix = (inputs_wide + mixed_wide * gate_open).astype(jnp.bfloat16)
    after_wide = after_mix.astype(jnp.float32)
    second_inverse = inverse_rms(after_wide)
    second_normed = after_wide * second_inverse
    mlp_input = (
        (second_normed * mlp_gain).astype(jnp.bfloat16).reshape(rows_local, mlp_blocks, block_in)
    )
    pre_gate = jnp.einsum(
        "tkd,kdh->tkh", mlp_input, gate_weight, preferred_element_type=jnp.float32
    )
    pre_up = jnp.einsum("tkd,kdh->tkh", mlp_input, up_weight, preferred_element_type=jnp.float32)
    sig_gate = jax.nn.sigmoid(pre_gate)
    hidden = (pre_gate * sig_gate * pre_up).astype(jnp.bfloat16)
    permuted = jnp.transpose(hidden, (0, 2, 1)).reshape(rows_local, mlp_blocks, block_hidden)
    upstream_wide = upstream.astype(jnp.float32)
    upstream_blocks = upstream.reshape(rows_local, mlp_blocks, block_in)
    grad_perm = jnp.einsum(
        "tkd,kdh->tkh", upstream_blocks, down_weight, preferred_element_type=jnp.float32
    ).astype(jnp.bfloat16)
    grad_hidden = jnp.transpose(
        grad_perm.reshape(rows_local, block_hidden, mlp_blocks), (0, 2, 1)
    ).astype(jnp.float32)
    grad_gate_pre = (grad_hidden * pre_up * sig_gate * (1.0 + pre_gate * (1.0 - sig_gate))).astype(
        jnp.bfloat16
    )
    grad_up_pre = (grad_hidden * pre_gate * sig_gate).astype(jnp.bfloat16)
    grad_inner = jnp.einsum(
        "tkh,kdh->tkd", grad_gate_pre, gate_weight, preferred_element_type=jnp.float32
    )
    grad_inner = grad_inner + jnp.einsum(
        "tkh,kdh->tkd", grad_up_pre, up_weight, preferred_element_type=jnp.float32
    )
    grad_inner = grad_inner.reshape(rows_local, width)
    grad_after = (
        upstream_wide + norm_backward(grad_inner * mlp_gain, second_normed, second_inverse)
    ).astype(jnp.bfloat16)
    grad_after_wide = grad_after.astype(jnp.float32)
    grad_mixed = (grad_after_wide * gate_open).astype(jnp.bfloat16)
    grad_open = grad_after_wide * mixed_wide * gate_open * (1.0 - gate_open)
    grad_mixed_cols = lax.all_to_all(
        grad_mixed.reshape(local_blocks, block_size, width),
        "seq",
        split_axis=1,
        concat_axis=0,
        tiled=True,
    )
    grad_section_cols = jnp.einsum(
        "cib,cid->bid", second_factor, grad_mixed_cols, preferred_element_type=jnp.float32
    ).astype(jnp.bfloat16)
    second_term = jnp.einsum(
        "cid,bid->cib", grad_mixed_cols, section_cols, preferred_element_type=jnp.float32
    )
    grad_section = lax.all_to_all(grad_section_cols, "seq", split_axis=0, concat_axis=1, tiled=True)
    first_term = jnp.einsum(
        "bid,bjd->bij", grad_section, blocked, preferred_element_type=jnp.float32
    )
    grad_normed = jnp.einsum(
        "bij,bid->bjd", first_factor, grad_section, preferred_element_type=jnp.float32
    ).reshape(rows_local, width)
    grad_normed = grad_normed + grad_open * gate_scale
    grad_inputs = (
        grad_after_wide + norm_backward(grad_normed * norm_gain, first_normed, first_inverse)
    ).astype(jnp.bfloat16)
    factor_first, factor_second = (
        lax.psum_scatter(
            first_term.astype(jnp.bfloat16), "dp", scatter_dimension=2, tiled=True
        ).astype(jnp.float32),
        lax.psum_scatter(
            second_term.astype(jnp.bfloat16), "dp", scatter_dimension=2, tiled=True
        ).astype(jnp.float32),
    )
    replicas = lax.axis_size("dp")
    factor_weight = (replicas * width) ** (-0.5)
    mlp_weight = (replicas * rows_local * lax.axis_size("seq")) ** (-0.5)
    gate_term = jnp.einsum(
        "tkd,tkh->kdh", mlp_input, grad_gate_pre, preferred_element_type=jnp.float32
    )
    up_term = jnp.einsum("tkd,tkh->kdh", mlp_input, grad_up_pre, preferred_element_type=jnp.float32)
    down_term = jnp.einsum(
        "tkd,tkh->kdh", upstream_blocks, permuted, preferred_element_type=jnp.float32
    )
    stacked = jnp.concatenate([gate_term, up_term, down_term], axis=1)
    seq_summed = lax.psum_scatter(stacked, "seq", scatter_dimension=2, tiled=True)
    reduced = lax.psum_scatter(seq_summed, "dp", scatter_dimension=0, tiled=True)
    reduced = reduced * mlp_weight
    grad_gate = reduced[:, 0:block_in, :]
    grad_up = reduced[:, block_in : 2 * block_in, :]
    grad_down = reduced[:, 2 * block_in : 3 * block_in, :]
    return (
        grad_inputs[None],
        factor_first * factor_weight,
        factor_second * factor_weight,
        grad_gate,
        grad_up,
        grad_down,
    )


MESH = pl.DeviceIdType.MESH
F32 = jnp.float32
BF16 = jnp.bfloat16
ROWS = 16


def mm(a, b, da=1, db=0):
    return lax.dot_general(a, b, (((da,), (db,)), ((), ())), preferred_element_type=F32)


def row_loop(total, step, fn):
    def one(n, carry):
        fn(pl.ds(pl.multiple_of(n * step, step), step))
        return carry

    lax.fori_loop(0, total // step, one, 0, unroll=2)


def count_loop(total, fn):
    def one(n, carry):
        fn(n)
        return carry

    lax.fori_loop(0, total, one, 0)


def fused(
    S, DP,
    tok, cot_in, ff, sf, gain1, scale1, bias1, gain2, gw_in, uw_in, dw_in,
    gtok, facs, wout,
    normed, sec_out, sec_cols, mc_out, mixed, opened, gm_out, gm_cols, gs_out, gs,
    mix, mix_t, onehot, w2, gh, hid, gg, gu, pg, pu, inner, norm2, inv2s, ginner, gos, gres,
    cot, gw, uw, dw, cotp, ws, rc, rx, xo, yo, ry, sz, rz, ft, rf,
    send, recv, csend, crecv, xsend, xrecv, ysend, yrecv, zsend, zrecv, fsend, frecv, lsem,
):
    me = lax.axis_index("seq")
    dp = lax.axis_index("dp")
    core = lax.rem(dp, 2)
    peer_core = dp + 1 - 2 * core
    peer_x = lax.rem(dp + 2, DP)
    rows, width = tok.shape
    K, E, H = gw.shape
    chunk = H // K
    ic = rows // S
    hs = H // S
    nbd = S // DP
    kd = K // DP
    half = rows // 2
    part = ic // 2
    ZS = S // 2
    yy = lax.rem(me, 2)
    zz = lax.div(me, 2)

    loads = []
    for n, (a, b) in enumerate(((cot_in, cot), (dw_in, dw), (gw_in, gw), (uw_in, uw))):
        load = pltpu.make_async_copy(a, b, lsem.at[n])
        load.start()
        loads.append(load)
    barrier = pltpu.get_barrier_semaphore()
    for r in range(1, S):
        pl.semaphore_signal(barrier, inc=1, device_id={"seq": lax.rem(me + r, S)}, device_id_type=MESH)
    for r in range(1, DP):
        pl.semaphore_signal(barrier, inc=1, device_id={"dp": lax.rem(dp + r, DP)}, device_id_type=MESH)

    def first_norm(s):
        v = tok[s, :].astype(F32)
        inv = lax.rsqrt(jnp.mean(v * v, axis=-1, keepdims=True) + epsilon)
        normed[s, :] = (v * inv * gain1[...]).astype(BF16)

    row_loop(rows, ROWS, first_norm)
    sec_out[...] = mm(ff[...], normed[...]).astype(BF16)
    pl.semaphore_wait(barrier, S - 1 + DP - 1)

    def aligned(start):
        return pl.ds(pl.multiple_of(start, part), part)

    def exchange(phase, h, src, dst):
        def where(ref, q):
            if len(ref.shape) == 3:
                return ref.at[h, aligned(q * part)]
            return ref.at[aligned(q * ic + h * part)]

        copies = []
        for r in range(1, S):
            q = lax.rem(me + r, S)
            cp = pltpu.make_async_remote_copy(
                src_ref=where(src, q),
                dst_ref=where(dst, me),
                send_sem=send.at[phase, h, r],
                recv_sem=recv.at[phase, h, r],
                device_id={"seq": q},
                device_id_type=MESH,
            )
            cp.start()
            copies.append(cp)
        where(dst, me)[...] = where(src, me)[...]
        return copies

    pending = []
    one = [exchange(0, h, sec_out, sec_cols) for h in range(2)]
    pending += one[0] + one[1]

    def open_gate(s):
        opened[s, :] = jax.nn.sigmoid(normed[s, :].astype(F32) * scale1[...] + bias1[...])

    row_loop(rows, ROWS, open_gate)
    ri = lax.broadcasted_iota(jnp.int32, (half, half), 0)
    ci = lax.broadcasted_iota(jnp.int32, (half, half), 1)
    same = lax.rem(ri, part) == lax.rem(ci, part)
    er = lax.broadcasted_iota(jnp.int32, (half, S), 0)
    ec = lax.broadcasted_iota(jnp.int32, (half, S), 1)
    expand = jnp.where(lax.div(er, part) == ec, 1.0, 0.0).astype(BF16)
    pi = lax.broadcasted_iota(jnp.int32, (part, half), 0)
    pj = lax.rem(lax.broadcasted_iota(jnp.int32, (part, half), 1), part)
    for c in range(S):
        spread_c = mm(sf[c], expand, 0, 1)
        for h in range(2):
            rows_c = jnp.where(pi == pj, spread_c[h * part : (h + 1) * part, :], 0.0)
            mix[h, c * part : (c + 1) * part, :] = rows_c.astype(BF16)
    for h in range(2):
        mix_t[h] = jnp.transpose(mix[h].astype(F32)).astype(BF16)

    def regroup(n):
        for h in range(2):
            cotp[aligned(h * half + n * part), :] = cot[aligned(n * ic + h * part), :]

    loads[0].wait()
    count_loop(S, regroup)

    def hot_rows(s):
        hi = lax.broadcasted_iota(jnp.int32, (ROWS, K * 128), 0) + s.start
        hc = lax.broadcasted_iota(jnp.int32, (ROWS, K * 128), 1)
        lane = lax.rem(hc, 128)
        hit = hi == lax.rem(lane, chunk) * K + lax.div(hc, 128)
        for r in range(2):
            onehot[r, s, :] = jnp.where(hit & (lax.div(lane, chunk) == r), 1.0, 0.0).astype(BF16)

    row_loop(H, ROWS, hot_rows)

    def spread(p):
        for r in range(2):
            w2[p, r * E : (r + 1) * E, :] = mm(dw[2 * p + r], onehot[r]).astype(BF16)

    loads[1].wait()
    count_loop(K // 2, spread)
    two = []
    for h in range(2):
        for cp in one[h]:
            cp.wait_recv()
        mc_out[h] = mm(mix[h], sec_cols[h]).astype(BF16)
        two.append(exchange(1, h, mc_out, mixed))
    pending += two[0] + two[1]

    def hidden_grad(p):
        g = mm(cotp[:, pl.ds(pl.multiple_of(p * 2 * E, 2 * E), 2 * E)], w2[p]).astype(BF16)
        for k in range(K):
            gh[k, :, pl.ds(pl.multiple_of(p * 128, 128), 128)] = g[:, k * 128 : (k + 1) * 128]

    count_loop(K // 2, hidden_grad)
    def second_norm(h, n):
        nat, own = aligned(n * ic + h * part), aligned(n * part)
        s = aligned(h * half + n * part)
        resid = (tok[nat, :].astype(F32) + mixed[h, own, :].astype(F32) * opened[nat, :]).astype(BF16).astype(F32)
        inv = lax.rsqrt(jnp.mean(resid * resid, axis=-1, keepdims=True) + epsilon)
        n2 = resid * inv
        norm2[s, :] = n2
        inv2s[s, :] = jnp.broadcast_to(inv, (part, 128))
        inner[s, :] = (n2 * gain2[...]).astype(BF16)

    def mlp(h, k):
        cols = pl.ds(pl.multiple_of(k * E, E), E)
        mine = slice(h * half, (h + 1) * half)
        x = inner[mine, cols]
        pg[...] = mm(x, gw[k])
        pu[...] = mm(x, uw[k])

        def act(s):
            a = pg[s, :]
            u = pu[s, :]
            t = pl.ds(pl.multiple_of(s.start + h * half, ROWS), ROWS)
            g = gh[k, t, :].astype(F32)
            sig = 0.5 * jnp.tanh(0.5 * a) + 0.5
            silu = a * sig
            hid[k, t, :] = (silu * u).astype(BF16)
            gg[k, t, :] = (g * u * (sig + silu * (1.0 - sig))).astype(BF16)
            gu[k, t, :] = (g * silu).astype(BF16)

        row_loop(half, ROWS, act)
        ginner[mine, cols] = mm(gg[k, mine, :], gw[k], 1, 1) + mm(gu[k, mine, :], uw[k], 1, 1)

    def second_back(h, n):
        nat, own = aligned(n * ic + h * part), aligned(n * part)
        s = aligned(h * half + n * part)
        n2 = norm2[s, :]
        dn = ginner[s, :] * gain2[...]
        mean = jnp.mean(dn * n2, axis=-1, keepdims=True)
        gr = (cot[nat, :].astype(F32) + inv2s[s, 0:1] * (dn - n2 * mean)).astype(BF16)
        gres[nat, :] = gr
        wide = gr.astype(F32)
        op = opened[nat, :]
        gm_out[h, own, :] = (wide * op).astype(BF16)
        gos[nat, :] = wide * mixed[h, own, :].astype(F32) * op * (1.0 - op) * scale1[...]

    loads[2].wait()
    loads[3].wait()
    three = []
    for h in range(2):
        for cp in two[h]:
            cp.wait_recv()
        count_loop(S, lambda n: second_norm(h, n))
        count_loop(K, lambda k: mlp(h, k))
        count_loop(S, lambda n: second_back(h, n))
        three.append(exchange(2, h, gm_out, gm_cols))
    pending += three[0] + three[1]

    def back_mix(h):
        for cp in three[h]:
            cp.wait_recv()
        gs_out[h] = mm(mix_t[h], gm_cols[h]).astype(BF16)
        return exchange(3, h, gs_out, gs)

    four = back_mix(0)

    def reach(j, slot, owner):
        cp = pltpu.make_async_remote_copy(
            src_ref=ws.at[j, owner],
            dst_ref=rc.at[j, slot],
            send_sem=csend.at[j, slot],
            recv_sem=crecv.at[j, slot],
            device_id={"dp": peer_core},
            device_id_type=MESH,
        )
        cp.start()
        return cp

    far_mine = lax.rem(dp + 2, DP)
    far_peer = lax.rem(peer_core + 2, DP)
    to_core = []

    def down_term(p):
        for r in range(2):
            c = cotp[:, pl.ds(pl.multiple_of((2 * p + r) * E, E), E)]
            parts = []
            for k in range(K):
                raw = mm(hid[k, :, pl.ds(pl.multiple_of(p * 128, 128), 128)], c, 0, 0)
                parts.append(raw[r * chunk : (r + 1) * chunk, :])
            size = chunk // S
            for q in range(S):
                piece = jnp.concatenate([v[q * size : (q + 1) * size, :] for v in parts], axis=0)
                ws[0, p, (q % 2) * ZS + q // 2, r * hs : (r + 1) * hs, :] = piece.astype(BF16)

    to_x = []

    def over_x(j):
        to_core[j][0].wait_recv()

        def add_far(q):
            xo[j, q] = (ws[j, far_mine, q].astype(F32) + rc[j, 0, q].astype(F32)).astype(BF16)

        count_loop(S, add_far)
        cp = pltpu.make_async_remote_copy(
            src_ref=xo.at[j],
            dst_ref=rx.at[j],
            send_sem=xsend.at[j],
            recv_sem=xrecv.at[j],
            device_id={"dp": peer_x},
            device_id_type=MESH,
        )
        cp.start()
        to_x.append(cp)

    count_loop(K // 2, down_term)
    to_core.append([reach(0, 0, far_peer), reach(0, 1, peer_core)])
    for j, grads in ((1, gg), (2, gu)):

        def in_term(p, j=j, grads=grads):
            for r in range(2):
                x = inner[:, pl.ds(pl.multiple_of((2 * p + r) * E, E), E)]
                raw = mm(grads[2 * p + r], x, 0, 0).astype(BF16)
                for q in range(S):
                    ws[j, p, (q % 2) * ZS + q // 2, r * hs : (r + 1) * hs, :] = raw[q * hs : (q + 1) * hs, :]

        count_loop(K // 2, in_term)
        to_core.append([reach(j, 0, far_peer), reach(j, 1, peer_core)])
        over_x(j - 1)

    four += back_mix(1)
    over_x(2)
    pending += four

    pr = lax.broadcasted_iota(jnp.int32, (DP * 16, half), 0)
    pc = lax.div(lax.broadcasted_iota(jnp.int32, (DP * 16, half), 1), part)
    pick = (lax.div(pr, 16) == lax.div(pc, nbd)) & (lax.rem(pr, 16) == lax.rem(pc, nbd))
    pick = jnp.where(pick, 1.0, 0.0).astype(BF16)
    share = rows // DP
    for h in range(2):
        outer = jnp.where(same, mm(sec_cols[h], gm_cols[h], 1, 1), 0.0).astype(BF16)
        picked = mm(pick, outer).astype(BF16)
        for d in range(DP):
            ft[d, share : share + 16, h * half : (h + 1) * half] = picked[d * 16 : (d + 1) * 16, :]

    to_y, to_z = [], []
    peer_y = me + 1 - 2 * yy

    def partial(j, q):
        return ws[j, dp, q].astype(F32) + rc[j, 1, q].astype(F32) + rx[j, q].astype(F32)

    def over_y(j):
        to_core[j][1].wait_recv()
        to_x[j].wait_recv()

        def add_far(z):
            yo[j, z] = partial(j, (1 - yy) * ZS + z).astype(BF16)

        count_loop(ZS, add_far)
        cp = pltpu.make_async_remote_copy(
            src_ref=yo.at[j],
            dst_ref=ry.at[j],
            send_sem=ysend.at[j],
            recv_sem=yrecv.at[j],
            device_id={"seq": peer_y},
            device_id_type=MESH,
        )
        cp.start()
        to_y.append(cp)

    def over_z(j):
        to_y[j].wait_recv()

        def add_own(z):
            sz[j, z] = (partial(j, yy * ZS + z) + ry[j, z].astype(F32)).astype(BF16)

        count_loop(ZS, add_own)
        for r in range(1, ZS):
            z = lax.rem(zz + r, ZS)
            cp = pltpu.make_async_remote_copy(
                src_ref=sz.at[j, z],
                dst_ref=rz.at[j, r],
                send_sem=zsend.at[j, r],
                recv_sem=zrecv.at[j, r],
                device_id={"seq": z * 2 + yy},
                device_id_type=MESH,
            )
            cp.start()
            to_z.append(cp)

    over_y(0)
    over_y(1)
    over_z(0)
    for cp in four:
        cp.wait_recv()
    f1 = mm(normed[...], gs[...], 1, 1).astype(BF16)
    for d in range(DP):
        ft[d, 0:share, :] = f1[d * share : (d + 1) * share, :]
    to_dp = []
    for r in range(1, DP):
        d = lax.rem(dp + r, DP)
        cp = pltpu.make_async_remote_copy(
            src_ref=ft.at[d],
            dst_ref=rf.at[r],
            send_sem=fsend.at[r],
            recv_sem=frecv.at[r],
            device_id={"dp": d},
            device_id_type=MESH,
        )
        cp.start()
        to_dp.append(cp)
    ginner[...] = mm(ff[...], gs[...], 0, 0)

    def first_back(s):
        v = tok[s, :].astype(F32)
        inv = lax.rsqrt(jnp.mean(v * v, axis=-1, keepdims=True) + epsilon)
        n1 = v * inv
        dm = (ginner[s, :] + gos[s, :]) * gain1[...]
        mean = jnp.mean(dm * n1, axis=-1, keepdims=True)
        gtok[s, :] = (gres[s, :].astype(F32) + inv * (dm - n1 * mean)).astype(BF16)

    over_y(2)
    over_z(1)
    row_loop(rows, ROWS, first_back)
    over_z(2)
    for cp in to_dp:
        cp.wait_recv()
    total = ft[dp].astype(F32)
    for r in range(1, DP):
        total = total + rf[r].astype(F32)
    facs[...] = total * ((DP * width) ** (-0.5))
    for cp in to_z:
        cp.wait_recv()
    scale = (DP * rows * S) ** (-0.5)
    for j in range(3):
        acc = sz[j, zz].astype(F32)
        for r in range(1, ZS):
            acc = acc + rz[j, r].astype(F32)
        wout[j] = acc * scale
    for cp in pending + to_y + to_z + to_x + to_dp + to_core[0] + to_core[1] + to_core[2]:
        cp.wait_send()


def arrange(S, share, part, kd, step, gtok_in, facs, wout, gtok, first, second, gate, up, down, sem):
    copy = pltpu.make_async_copy(gtok_in, gtok, sem)
    copy.start()
    first[...] = facs[0:share, :]
    nbd = second.shape[1]
    half = S * part
    for c in range(S):
        pieces = [facs[share : share + nbd, h * half + c * part : h * half + (c + 1) * part] for h in range(2)]
        second[c] = jnp.concatenate(pieces, axis=1)
    gate[...] = wout[1]
    up[...] = wout[2]
    size = wout.shape[1] // kd
    K = size // step
    for d in range(kd):
        for k in range(K):
            at = d * size + k * step
            down[pl.ds(d * size + k, step, stride=K), :] = wout[0, at : at + step, :]
    copy.wait()


def fused_body(
    tokens, cotangent, first_factor, second_factor, norm_gain, gate_scale, gate_bias, mlp_gain,
    gate_weight, up_weight, down_weight,
):
    S, DP = lax.axis_size("seq"), lax.axis_size("dp")
    rows, width = tokens.shape[1:]
    K, E, H = gate_weight.shape
    ic = rows // S
    nbd = S // DP
    hs = H // S
    kd = K // DP
    share = rows // DP
    part = ic // 2
    split = jnp.transpose(second_factor, (0, 2, 1))
    gains = [v.reshape(1, width) for v in (norm_gain, gate_scale, gate_bias, mlp_gain)]
    full = (rows, width)
    vm = pltpu.VMEM
    wide = vm(full, F32)
    half = vm(full, BF16)
    pair = vm((2, rows // 2, width), BF16)
    deep = vm((K, rows, H), BF16)
    dma = pltpu.SemaphoreType.DMA
    scratch = [
        half, half, pair, pair, pair, wide, pair, pair, pair, half,
        vm((2, rows // 2, rows // 2), BF16), vm((2, rows // 2, rows // 2), BF16), vm((2, H, K * 128), BF16),
        vm((K // 2, 2 * E, K * 128), BF16), deep, deep, deep, deep,
        vm((rows // 2, H), F32), vm((rows // 2, H), F32), half, wide, vm((rows, 128), F32), wide, wide, half,
        half, vm((K, E, H), BF16), vm((K, E, H), BF16), vm((K, E, H), BF16),
        half, vm((3, DP, S, kd * hs, E), BF16), vm((3, 2, S, kd * hs, E), BF16),
        vm((3, S, kd * hs, E), BF16), vm((3, S, kd * hs, E), BF16),
        vm((3, S // 2, kd * hs, E), BF16), vm((3, S // 2, kd * hs, E), BF16),
        vm((3, S // 2, kd * hs, E), BF16), vm((3, S // 2, kd * hs, E), BF16),
        vm((DP, share + 16, rows), BF16), vm((DP, share + 16, rows), BF16),
        dma((4, 2, S)), dma((4, 2, S)), dma((3, 2)), dma((3, 2)), dma((3,)), dma((3,)),
        dma((3,)), dma((3,)), dma((3, S // 2)), dma((3, S // 2)), dma((DP,)), dma((DP,)), dma((4,)),
    ]
    whole = pl.BlockSpec(memory_space=pltpu.VMEM)
    away = pl.BlockSpec(memory_space=pl.ANY)
    gtok, facs, wout = pl.pallas_call(
        lambda *refs: fused(S, DP, *refs),
        out_shape=(
            jax.ShapeDtypeStruct(full, BF16),
            jax.ShapeDtypeStruct((share + 16, rows), F32),
            jax.ShapeDtypeStruct((3, kd * hs, E), F32),
        ),
        in_specs=[whole, away] + [whole] * 6 + [away] * 3,
        out_specs=(whole,) * 3,
        scratch_shapes=scratch,
        compiler_params=pltpu.CompilerParams(
            collective_id=0, has_side_effects=True, vmem_limit_bytes=62 * 1024 * 1024
        ),
    )(tokens[0], cotangent[0], first_factor[0], split, *gains, gate_weight, up_weight, down_weight)
    outs = pl.pallas_call(
        lambda *refs: arrange(S, share, part, kd, hs // K, *refs),
        out_shape=(
            jax.ShapeDtypeStruct(full, BF16),
            jax.ShapeDtypeStruct((share, rows), F32),
            jax.ShapeDtypeStruct((S, nbd, ic), F32),
            jax.ShapeDtypeStruct((kd * hs, E), F32),
            jax.ShapeDtypeStruct((kd * hs, E), F32),
            jax.ShapeDtypeStruct((kd * hs, E), F32),
        ),
        in_specs=[away, whole, whole],
        out_specs=(away,) + (whole,) * 5,
        scratch_shapes=[dma(())],
    )(gtok, facs, wout)
    gtok, first, second, gate, up, down = outs
    gate, up, down = [jnp.transpose(w.reshape(kd, hs, E), (0, 2, 1)) for w in (gate, up, down)]
    return gtok[None], first.T[None], jnp.transpose(second, (0, 2, 1)), gate, up, down


def body(*args):
    S, DP = lax.axis_size("seq"), lax.axis_size("dp")
    blocks, rows = args[2].shape[:2]
    K, E, H = args[8].shape
    fits = (
        blocks == 1 and args[0].shape[0] == 1 and args[0].shape[1] == rows and rows == S * 2 * ROWS
        and DP == 4 and S % DP == 0 and S // DP <= 16 and S <= 128
        and E == 128 and H == K * 64 and K == 2 * DP and 64 % (8 * S) == 0
    )
    return fused_body(*args) if fits else plain_body(*args)


def solution(mesh):
    placed = (
        P("dp", "seq", None),
        P("dp", "seq", None),
        P("seq", None, None),
        P(None, "seq", None),
        P(),
        P(),
        P(),
        P(),
        P(),
        P(),
        P(),
    )
    return jax.shard_map(
        body,
        mesh=mesh,
        in_specs=placed,
        out_specs=(
            P("dp", "seq", None),
            P("seq", None, "dp"),
            P(None, "seq", "dp"),
            P("dp", None, "seq"),
            P("dp", None, "seq"),
            P("dp", None, "seq"),
        ),
        check_vma=False,
    )
```

```python
import jax
import jax.numpy as jnp
from jax import lax
from jax.experimental import pallas as pl
from jax.experimental.pallas import tpu as pltpu
from jax.sharding import PartitionSpec as P

epsilon = 1e-05


def inverse_rms(values):
    return lax.rsqrt(jnp.mean(values * values, axis=-1, keepdims=True) + epsilon)


def norm_backward(grad_normed, normed_values, inverse):
    return inverse * (
        grad_normed - normed_values * jnp.mean(grad_normed * normed_values, axis=-1, keepdims=True)
    )


def plain_body(
    tokens,
    cotangent,
    first_factor,
    second_factor,
    norm_gain,
    gate_scale,
    gate_bias,
    mlp_gain,
    gate_weight,
    up_weight,
    down_weight,
):
    inputs = tokens[0]
    upstream = cotangent[0]
    rows_local, width = inputs.shape
    local_blocks, block_size = (first_factor.shape[0], first_factor.shape[1])
    mlp_blocks, block_in, block_hidden = gate_weight.shape
    inputs_wide = inputs.astype(jnp.float32)
    first_inverse = inverse_rms(inputs_wide)
    first_normed = inputs_wide * first_inverse
    normed_tokens = (first_normed * norm_gain).astype(jnp.bfloat16)
    blocked = normed_tokens.reshape(local_blocks, block_size, width)
    section_one = jnp.einsum(
        "bij,bjd->bid", first_factor, blocked, preferred_element_type=jnp.float32
    ).astype(jnp.bfloat16)
    section_cols = lax.all_to_all(section_one, "seq", split_axis=1, concat_axis=0, tiled=True)
    mixed_cols = jnp.einsum(
        "cib,bid->cid", second_factor, section_cols, preferred_element_type=jnp.float32
    ).astype(jnp.bfloat16)
    mixed_rows = lax.all_to_all(mixed_cols, "seq", split_axis=0, concat_axis=1, tiled=True).reshape(
        rows_local, width
    )
    mixed_wide = mixed_rows.astype(jnp.float32)
    gate_open = jax.nn.sigmoid(normed_tokens.astype(jnp.float32) * gate_scale + gate_bias)
    after_mix = (inputs_wide + mixed_wide * gate_open).astype(jnp.bfloat16)
    after_wide = after_mix.astype(jnp.float32)
    second_inverse = inverse_rms(after_wide)
    second_normed = after_wide * second_inverse
    mlp_input = (
        (second_normed * mlp_gain).astype(jnp.bfloat16).reshape(rows_local, mlp_blocks, block_in)
    )
    pre_gate = jnp.einsum(
        "tkd,kdh->tkh", mlp_input, gate_weight, preferred_element_type=jnp.float32
    )
    pre_up = jnp.einsum("tkd,kdh->tkh", mlp_input, up_weight, preferred_element_type=jnp.float32)
    sig_gate = jax.nn.sigmoid(pre_gate)
    hidden = (pre_gate * sig_gate * pre_up).astype(jnp.bfloat16)
    permuted = jnp.transpose(hidden, (0, 2, 1)).reshape(rows_local, mlp_blocks, block_hidden)
    upstream_wide = upstream.astype(jnp.float32)
    upstream_blocks = upstream.reshape(rows_local, mlp_blocks, block_in)
    grad_perm = jnp.einsum(
        "tkd,kdh->tkh", upstream_blocks, down_weight, preferred_element_type=jnp.float32
    ).astype(jnp.bfloat16)
    grad_hidden = jnp.transpose(
        grad_perm.reshape(rows_local, block_hidden, mlp_blocks), (0, 2, 1)
    ).astype(jnp.float32)
    grad_gate_pre = (grad_hidden * pre_up * sig_gate * (1.0 + pre_gate * (1.0 - sig_gate))).astype(
        jnp.bfloat16
    )
    grad_up_pre = (grad_hidden * pre_gate * sig_gate).astype(jnp.bfloat16)
    grad_inner = jnp.einsum(
        "tkh,kdh->tkd", grad_gate_pre, gate_weight, preferred_element_type=jnp.float32
    )
    grad_inner = grad_inner + jnp.einsum(
        "tkh,kdh->tkd", grad_up_pre, up_weight, preferred_element_type=jnp.float32
    )
    grad_inner = grad_inner.reshape(rows_local, width)
    grad_after = (
        upstream_wide + norm_backward(grad_inner * mlp_gain, second_normed, second_inverse)
    ).astype(jnp.bfloat16)
    grad_after_wide = grad_after.astype(jnp.float32)
    grad_mixed = (grad_after_wide * gate_open).astype(jnp.bfloat16)
    grad_open = grad_after_wide * mixed_wide * gate_open * (1.0 - gate_open)
    grad_mixed_cols = lax.all_to_all(
        grad_mixed.reshape(local_blocks, block_size, width),
        "seq",
        split_axis=1,
        concat_axis=0,
        tiled=True,
    )
    grad_section_cols = jnp.einsum(
        "cib,cid->bid", second_factor, grad_mixed_cols, preferred_element_type=jnp.float32
    ).astype(jnp.bfloat16)
    second_term = jnp.einsum(
        "cid,bid->cib", grad_mixed_cols, section_cols, preferred_element_type=jnp.float32
    )
    grad_section = lax.all_to_all(grad_section_cols, "seq", split_axis=0, concat_axis=1, tiled=True)
    first_term = jnp.einsum(
        "bid,bjd->bij", grad_section, blocked, preferred_element_type=jnp.float32
    )
    grad_normed = jnp.einsum(
        "bij,bid->bjd", first_factor, grad_section, preferred_element_type=jnp.float32
    ).reshape(rows_local, width)
    grad_normed = grad_normed + grad_open * gate_scale
    grad_inputs = (
        grad_after_wide + norm_backward(grad_normed * norm_gain, first_normed, first_inverse)
    ).astype(jnp.bfloat16)
    factor_first, factor_second = (
        lax.psum_scatter(
            first_term.astype(jnp.bfloat16), "dp", scatter_dimension=2, tiled=True
        ).astype(jnp.float32),
        lax.psum_scatter(
            second_term.astype(jnp.bfloat16), "dp", scatter_dimension=2, tiled=True
        ).astype(jnp.float32),
    )
    replicas = lax.axis_size("dp")
    factor_weight = (replicas * width) ** (-0.5)
    mlp_weight = (replicas * rows_local * lax.axis_size("seq")) ** (-0.5)
    gate_term = jnp.einsum(
        "tkd,tkh->kdh", mlp_input, grad_gate_pre, preferred_element_type=jnp.float32
    )
    up_term = jnp.einsum("tkd,tkh->kdh", mlp_input, grad_up_pre, preferred_element_type=jnp.float32)
    down_term = jnp.einsum(
        "tkd,tkh->kdh", upstream_blocks, permuted, preferred_element_type=jnp.float32
    )
    stacked = jnp.concatenate([gate_term, up_term, down_term], axis=1)
    seq_summed = lax.psum_scatter(stacked, "seq", scatter_dimension=2, tiled=True)
    reduced = lax.psum_scatter(seq_summed, "dp", scatter_dimension=0, tiled=True)
    reduced = reduced * mlp_weight
    grad_gate = reduced[:, 0:block_in, :]
    grad_up = reduced[:, block_in : 2 * block_in, :]
    grad_down = reduced[:, 2 * block_in : 3 * block_in, :]
    return (
        grad_inputs[None],
        factor_first * factor_weight,
        factor_second * factor_weight,
        grad_gate,
        grad_up,
        grad_down,
    )


MESH = pl.DeviceIdType.MESH
F32 = jnp.float32
BF16 = jnp.bfloat16
ROWS = 16


def mm(a, b, da=1, db=0):
    return lax.dot_general(a, b, (((da,), (db,)), ((), ())), preferred_element_type=F32)


def row_loop(total, step, fn):
    def one(n, carry):
        fn(pl.ds(pl.multiple_of(n * step, step), step))
        return carry

    lax.fori_loop(0, total // step, one, 0, unroll=2)


def count_loop(total, fn):
    def one(n, carry):
        fn(n)
        return carry

    lax.fori_loop(0, total, one, 0)


def fused(
    S, DP,
    tok, cot_in, ff, sf, gain1, scale1, bias1, gain2, gw_in, uw_in, dw_in,
    gtok, facs, wout,
    normed, sec_out, sec_cols, mc_out, mixed, opened, gm_out, gm_cols, gs_out, gs,
    mix, mix_t, onehot, w2, gh, hid, gg, gu, pg, pu, inner, norm2, inv2s, ginner, gos, gres,
    cot, gw, uw, dw, cotp, ws, rc, rx, xo, yo, ry, sz, rz, ft, rf,
    send, recv, csend, crecv, xsend, xrecv, ysend, yrecv, zsend, zrecv, fsend, frecv, lsem,
):
    me = lax.axis_index("seq")
    dp = lax.axis_index("dp")
    core = lax.rem(dp, 2)
    peer_core = dp + 1 - 2 * core
    peer_x = lax.rem(dp + 2, DP)
    rows, width = tok.shape
    K, E, H = gw.shape
    chunk = H // K
    ic = rows // S
    hs = H // S
    nbd = S // DP
    kd = K // DP
    half = rows // 2
    part = ic // 2
    ZS = S // 2
    yy = lax.rem(me, 2)
    zz = lax.div(me, 2)

    loads = []
    for n, (a, b) in enumerate(((cot_in, cot), (dw_in, dw), (gw_in, gw), (uw_in, uw))):
        load = pltpu.make_async_copy(a, b, lsem.at[n])
        load.start()
        loads.append(load)
    barrier = pltpu.get_barrier_semaphore()
    for r in range(1, S):
        pl.semaphore_signal(barrier, inc=1, device_id={"seq": lax.rem(me + r, S)}, device_id_type=MESH)
    for r in range(1, DP):
        pl.semaphore_signal(barrier, inc=1, device_id={"dp": lax.rem(dp + r, DP)}, device_id_type=MESH)

    def first_norm(s):
        v = tok[s, :].astype(F32)
        inv = lax.rsqrt(jnp.mean(v * v, axis=-1, keepdims=True) + epsilon)
        normed[s, :] = (v * inv * gain1[...]).astype(BF16)

    row_loop(rows, ROWS, first_norm)
    sec_out[...] = mm(ff[...], normed[...]).astype(BF16)
    pl.semaphore_wait(barrier, S - 1 + DP - 1)

    def aligned(start):
        return pl.ds(pl.multiple_of(start, part), part)

    def exchange(phase, h, src, dst):
        def where(ref, q):
            if len(ref.shape) == 3:
                return ref.at[h, aligned(q * part)]
            return ref.at[aligned(q * ic + h * part)]

        copies = []
        for r in range(1, S):
            q = lax.rem(me + r, S)
            cp = pltpu.make_async_remote_copy(
                src_ref=where(src, q),
                dst_ref=where(dst, me),
                send_sem=send.at[phase, h, r],
                recv_sem=recv.at[phase, h, r],
                device_id={"seq": q},
                device_id_type=MESH,
            )
            cp.start()
            copies.append(cp)
        where(dst, me)[...] = where(src, me)[...]
        return copies

    pending = []
    one = [exchange(0, h, sec_out, sec_cols) for h in range(2)]
    pending += one[0] + one[1]

    def open_gate(s):
        opened[s, :] = jax.nn.sigmoid(normed[s, :].astype(F32) * scale1[...] + bias1[...])

    row_loop(rows, ROWS, open_gate)
    ri = lax.broadcasted_iota(jnp.int32, (half, half), 0)
    ci = lax.broadcasted_iota(jnp.int32, (half, half), 1)
    same = lax.rem(ri, part) == lax.rem(ci, part)
    er = lax.broadcasted_iota(jnp.int32, (half, S), 0)
    ec = lax.broadcasted_iota(jnp.int32, (half, S), 1)
    expand = jnp.where(lax.div(er, part) == ec, 1.0, 0.0).astype(BF16)
    pi = lax.broadcasted_iota(jnp.int32, (part, half), 0)
    pj = lax.rem(lax.broadcasted_iota(jnp.int32, (part, half), 1), part)
    for c in range(S):
        spread_c = mm(sf[c], expand, 0, 1)
        for h in range(2):
            rows_c = jnp.where(pi == pj, spread_c[h * part : (h + 1) * part, :], 0.0)
            mix[h, c * part : (c + 1) * part, :] = rows_c.astype(BF16)
    for h in range(2):
        mix_t[h] = jnp.transpose(mix[h].astype(F32)).astype(BF16)

    def regroup(n):
        for h in range(2):
            cotp[aligned(h * half + n * part), :] = cot[aligned(n * ic + h * part), :]

    loads[0].wait()
    count_loop(S, regroup)

    def hot_rows(s):
        hi = lax.broadcasted_iota(jnp.int32, (ROWS, K * 128), 0) + s.start
        hc = lax.broadcasted_iota(jnp.int32, (ROWS, K * 128), 1)
        lane = lax.rem(hc, 128)
        hit = hi == lax.rem(lane, chunk) * K + lax.div(hc, 128)
        for r in range(2):
            onehot[r, s, :] = jnp.where(hit & (lax.div(lane, chunk) == r), 1.0, 0.0).astype(BF16)

    row_loop(H, ROWS, hot_rows)

    def spread(p):
        for r in range(2):
            w2[p, r * E : (r + 1) * E, :] = mm(dw[2 * p + r], onehot[r]).astype(BF16)

    loads[1].wait()
    count_loop(K // 2, spread)
    two = []
    for h in range(2):
        for cp in one[h]:
            cp.wait_recv()
        mc_out[h] = mm(mix[h], sec_cols[h]).astype(BF16)
        two.append(exchange(1, h, mc_out, mixed))
    pending += two[0] + two[1]

    def hidden_grad(p):
        g = mm(cotp[:, pl.ds(pl.multiple_of(p * 2 * E, 2 * E), 2 * E)], w2[p]).astype(BF16)
        for k in range(K):
            gh[k, :, pl.ds(pl.multiple_of(p * 128, 128), 128)] = g[:, k * 128 : (k + 1) * 128]

    count_loop(K // 2, hidden_grad)
    def second_norm(h, n):
        nat, own = aligned(n * ic + h * part), aligned(n * part)
        s = aligned(h * half + n * part)
        resid = (tok[nat, :].astype(F32) + mixed[h, own, :].astype(F32) * opened[nat, :]).astype(BF16).astype(F32)
        inv = lax.rsqrt(jnp.mean(resid * resid, axis=-1, keepdims=True) + epsilon)
        n2 = resid * inv
        norm2[s, :] = n2
        inv2s[s, :] = jnp.broadcast_to(inv, (part, 128))
        inner[s, :] = (n2 * gain2[...]).astype(BF16)

    def mlp(h, k):
        cols = pl.ds(pl.multiple_of(k * E, E), E)
        mine = slice(h * half, (h + 1) * half)
        x = inner[mine, cols]
        pg[...] = mm(x, gw[k])
        pu[...] = mm(x, uw[k])

        def act(s):
            a = pg[s, :]
            u = pu[s, :]
            t = pl.ds(pl.multiple_of(s.start + h * half, ROWS), ROWS)
            g = gh[k, t, :].astype(F32)
            sig = 0.5 * jnp.tanh(0.5 * a) + 0.5
            silu = a * sig
            hid[k, t, :] = (silu * u).astype(BF16)
            gg[k, t, :] = (g * u * (sig + silu * (1.0 - sig))).astype(BF16)
            gu[k, t, :] = (g * silu).astype(BF16)

        row_loop(half, ROWS, act)
        ginner[mine, cols] = mm(gg[k, mine, :], gw[k], 1, 1) + mm(gu[k, mine, :], uw[k], 1, 1)

    def second_back(h, n):
        nat, own = aligned(n * ic + h * part), aligned(n * part)
        s = aligned(h * half + n * part)
        n2 = norm2[s, :]
        dn = ginner[s, :] * gain2[...]
        mean = jnp.mean(dn * n2, axis=-1, keepdims=True)
        gr = (cot[nat, :].astype(F32) + inv2s[s, 0:1] * (dn - n2 * mean)).astype(BF16)
        gres[nat, :] = gr
        wide = gr.astype(F32)
        op = opened[nat, :]
        gm_out[h, own, :] = (wide * op).astype(BF16)
        gos[nat, :] = wide * mixed[h, own, :].astype(F32) * op * (1.0 - op) * scale1[...]

    loads[2].wait()
    loads[3].wait()
    three = []
    for h in range(2):
        for cp in two[h]:
            cp.wait_recv()
        count_loop(S, lambda n: second_norm(h, n))
        count_loop(K, lambda k: mlp(h, k))
        count_loop(S, lambda n: second_back(h, n))
        three.append(exchange(2, h, gm_out, gm_cols))
    pending += three[0] + three[1]

    def back_mix(h):
        for cp in three[h]:
            cp.wait_recv()
        gs_out[h] = mm(mix_t[h], gm_cols[h]).astype(BF16)
        return exchange(3, h, gs_out, gs)

    four = back_mix(0)

    def reach(j, slot, owner):
        cp = pltpu.make_async_remote_copy(
            src_ref=ws.at[j, owner],
            dst_ref=rc.at[j, slot],
            send_sem=csend.at[j, slot],
            recv_sem=crecv.at[j, slot],
            device_id={"dp": peer_core},
            device_id_type=MESH,
        )
        cp.start()
        return cp

    far_mine = lax.rem(dp + 2, DP)
    far_peer = lax.rem(peer_core + 2, DP)
    to_core = []

    def down_term(p):
        for r in range(2):
            c = cotp[:, pl.ds(pl.multiple_of((2 * p + r) * E, E), E)]
            parts = []
            for k in range(K):
                raw = mm(hid[k, :, pl.ds(pl.multiple_of(p * 128, 128), 128)], c, 0, 0)
                parts.append(raw[r * chunk : (r + 1) * chunk, :])
            size = chunk // S
            for q in range(S):
                piece = jnp.concatenate([v[q * size : (q + 1) * size, :] for v in parts], axis=0)
                ws[0, p, (q % 2) * ZS + q // 2, r * hs : (r + 1) * hs, :] = piece.astype(BF16)

    to_x = []

    def over_x(j):
        to_core[j][0].wait_recv()

        def add_far(q):
            xo[j, q] = (ws[j, far_mine, q].astype(F32) + rc[j, 0, q].astype(F32)).astype(BF16)

        count_loop(S, add_far)
        cp = pltpu.make_async_remote_copy(
            src_ref=xo.at[j],
            dst_ref=rx.at[j],
            send_sem=xsend.at[j],
            recv_sem=xrecv.at[j],
            device_id={"dp": peer_x},
            device_id_type=MESH,
        )
        cp.start()
        to_x.append(cp)

    count_loop(K // 2, down_term)
    to_core.append([reach(0, 0, far_peer), reach(0, 1, peer_core)])
    for j, grads in ((1, gg), (2, gu)):

        def in_term(p, j=j, grads=grads):
            for r in range(2):
                x = inner[:, pl.ds(pl.multiple_of((2 * p + r) * E, E), E)]
                raw = mm(grads[2 * p + r], x, 0, 0).astype(BF16)
                for q in range(S):
                    ws[j, p, (q % 2) * ZS + q // 2, r * hs : (r + 1) * hs, :] = raw[q * hs : (q + 1) * hs, :]

        count_loop(K // 2, in_term)
        to_core.append([reach(j, 0, far_peer), reach(j, 1, peer_core)])
        over_x(j - 1)

    four += back_mix(1)
    over_x(2)
    pending += four

    pr = lax.broadcasted_iota(jnp.int32, (DP * 16, half), 0)
    pc = lax.div(lax.broadcasted_iota(jnp.int32, (DP * 16, half), 1), part)
    pick = (lax.div(pr, 16) == lax.div(pc, nbd)) & (lax.rem(pr, 16) == lax.rem(pc, nbd))
    pick = jnp.where(pick, 1.0, 0.0).astype(BF16)
    share = rows // DP
    for h in range(2):
        outer = jnp.where(same, mm(sec_cols[h], gm_cols[h], 1, 1), 0.0).astype(BF16)
        picked = mm(pick, outer).astype(BF16)
        for d in range(DP):
            ft[d, share : share + 16, h * half : (h + 1) * half] = picked[d * 16 : (d + 1) * 16, :]

    to_y, to_z = [], []
    peer_y = me + 1 - 2 * yy

    def partial(j, q):
        return ws[j, dp, q].astype(F32) + rc[j, 1, q].astype(F32) + rx[j, q].astype(F32)

    def over_y(j):
        to_core[j][1].wait_recv()
        to_x[j].wait_recv()

        def add_far(z):
            yo[j, z] = partial(j, (1 - yy) * ZS + z).astype(BF16)

        count_loop(ZS, add_far)
        cp = pltpu.make_async_remote_copy(
            src_ref=yo.at[j],
            dst_ref=ry.at[j],
            send_sem=ysend.at[j],
            recv_sem=yrecv.at[j],
            device_id={"seq": peer_y},
            device_id_type=MESH,
        )
        cp.start()
        to_y.append(cp)

    def over_z(j):
        to_y[j].wait_recv()

        def add_own(z):
            sz[j, z] = (partial(j, yy * ZS + z) + ry[j, z].astype(F32)).astype(BF16)

        count_loop(ZS, add_own)
        for r in range(1, ZS):
            z = lax.rem(zz + r, ZS)
            cp = pltpu.make_async_remote_copy(
                src_ref=sz.at[j, z],
                dst_ref=rz.at[j, r],
                send_sem=zsend.at[j, r],
                recv_sem=zrecv.at[j, r],
                device_id={"seq": z * 2 + yy},
                device_id_type=MESH,
            )
            cp.start()
            to_z.append(cp)

    over_y(0)
    over_y(1)
    over_z(0)
    for cp in four:
        cp.wait_recv()
    f1 = mm(normed[...], gs[...], 1, 1).astype(BF16)
    for d in range(DP):
        ft[d, 0:share, :] = f1[d * share : (d + 1) * share, :]
    to_dp = []
    for r in range(1, DP):
        d = lax.rem(dp + r, DP)
        cp = pltpu.make_async_remote_copy(
            src_ref=ft.at[d],
            dst_ref=rf.at[r],
            send_sem=fsend.at[r],
            recv_sem=frecv.at[r],
            device_id={"dp": d},
            device_id_type=MESH,
        )
        cp.start()
        to_dp.append(cp)
    ginner[...] = mm(ff[...], gs[...], 0, 0)

    def first_back(s):
        v = tok[s, :].astype(F32)
        inv = lax.rsqrt(jnp.mean(v * v, axis=-1, keepdims=True) + epsilon)
        n1 = v * inv
        dm = (ginner[s, :] + gos[s, :]) * gain1[...]
        mean = jnp.mean(dm * n1, axis=-1, keepdims=True)
        gtok[s, :] = (gres[s, :].astype(F32) + inv * (dm - n1 * mean)).astype(BF16)

    over_y(2)
    over_z(1)
    row_loop(rows, ROWS, first_back)
    over_z(2)
    for cp in to_dp:
        cp.wait_recv()
    total = ft[dp].astype(F32)
    for r in range(1, DP):
        total = total + rf[r].astype(F32)
    facs[...] = total * ((DP * width) ** (-0.5))
    for cp in to_z:
        cp.wait_recv()
    scale = (DP * rows * S) ** (-0.5)
    for j in range(3):
        acc = sz[j, zz].astype(F32)
        for r in range(1, ZS):
            acc = acc + rz[j, r].astype(F32)
        wout[j] = acc * scale
    for cp in pending + to_y + to_z + to_x + to_dp + to_core[0] + to_core[1] + to_core[2]:
        cp.wait_send()


def arrange(S, share, part, kd, step, gtok_in, facs, wout, gtok, first, second, gate, up, down):
    gtok[...] = gtok_in[...]
    first[...] = facs[0:share, :]
    nbd = second.shape[1]
    half = S * part
    for c in range(S):
        pieces = [facs[share : share + nbd, h * half + c * part : h * half + (c + 1) * part] for h in range(2)]
        second[c] = jnp.concatenate(pieces, axis=1)
    gate[...] = wout[1]
    up[...] = wout[2]
    size = wout.shape[1] // kd
    K = size // step
    for d in range(kd):
        for k in range(K):
            at = d * size + k * step
            down[pl.ds(d * size + k, step, stride=K), :] = wout[0, at : at + step, :]


def fused_body(
    tokens, cotangent, first_factor, second_factor, norm_gain, gate_scale, gate_bias, mlp_gain,
    gate_weight, up_weight, down_weight,
):
    S, DP = lax.axis_size("seq"), lax.axis_size("dp")
    rows, width = tokens.shape[1:]
    K, E, H = gate_weight.shape
    ic = rows // S
    nbd = S // DP
    hs = H // S
    kd = K // DP
    share = rows // DP
    part = ic // 2
    split = jnp.transpose(second_factor, (0, 2, 1))
    gains = [v.reshape(1, width) for v in (norm_gain, gate_scale, gate_bias, mlp_gain)]
    full = (rows, width)
    vm = pltpu.VMEM
    wide = vm(full, F32)
    half = vm(full, BF16)
    pair = vm((2, rows // 2, width), BF16)
    deep = vm((K, rows, H), BF16)
    dma = pltpu.SemaphoreType.DMA
    scratch = [
        half, half, pair, pair, pair, wide, pair, pair, pair, half,
        vm((2, rows // 2, rows // 2), BF16), vm((2, rows // 2, rows // 2), BF16), vm((2, H, K * 128), BF16),
        vm((K // 2, 2 * E, K * 128), BF16), deep, deep, deep, deep,
        vm((rows // 2, H), F32), vm((rows // 2, H), F32), half, wide, vm((rows, 128), F32), wide, wide, half,
        half, vm((K, E, H), BF16), vm((K, E, H), BF16), vm((K, E, H), BF16),
        half, vm((3, DP, S, kd * hs, E), BF16), vm((3, 2, S, kd * hs, E), BF16),
        vm((3, S, kd * hs, E), BF16), vm((3, S, kd * hs, E), BF16),
        vm((3, S // 2, kd * hs, E), BF16), vm((3, S // 2, kd * hs, E), BF16),
        vm((3, S // 2, kd * hs, E), BF16), vm((3, S // 2, kd * hs, E), BF16),
        vm((DP, share + 16, rows), BF16), vm((DP, share + 16, rows), BF16),
        dma((4, 2, S)), dma((4, 2, S)), dma((3, 2)), dma((3, 2)), dma((3,)), dma((3,)),
        dma((3,)), dma((3,)), dma((3, S // 2)), dma((3, S // 2)), dma((DP,)), dma((DP,)), dma((4,)),
    ]
    whole = pl.BlockSpec(memory_space=pltpu.VMEM)
    away = pl.BlockSpec(memory_space=pl.ANY)
    gtok, facs, wout = pl.pallas_call(
        lambda *refs: fused(S, DP, *refs),
        out_shape=(
            jax.ShapeDtypeStruct(full, BF16),
            jax.ShapeDtypeStruct((share + 16, rows), F32),
            jax.ShapeDtypeStruct((3, kd * hs, E), F32),
        ),
        in_specs=[whole, away] + [whole] * 6 + [away] * 3,
        out_specs=(whole,) * 3,
        scratch_shapes=scratch,
        compiler_params=pltpu.CompilerParams(
            collective_id=0, has_side_effects=True, vmem_limit_bytes=62 * 1024 * 1024
        ),
    )(tokens[0], cotangent[0], first_factor[0], split, *gains, gate_weight, up_weight, down_weight)
    outs = pl.pallas_call(
        lambda *refs: arrange(S, share, part, kd, hs // K, *refs),
        out_shape=(
            jax.ShapeDtypeStruct(full, BF16),
            jax.ShapeDtypeStruct((share, rows), F32),
            jax.ShapeDtypeStruct((S, nbd, ic), F32),
            jax.ShapeDtypeStruct((kd * hs, E), F32),
            jax.ShapeDtypeStruct((kd * hs, E), F32),
            jax.ShapeDtypeStruct((kd * hs, E), F32),
        ),
        in_specs=[whole] * 3,
        out_specs=(whole,) * 6,
    )(gtok, facs, wout)
    gtok, first, second, gate, up, down = outs
    gate, up, down = [jnp.transpose(w.reshape(kd, hs, E), (0, 2, 1)) for w in (gate, up, down)]
    return gtok[None], first.T[None], jnp.transpose(second, (0, 2, 1)), gate, up, down


def body(*args):
    S, DP = lax.axis_size("seq"), lax.axis_size("dp")
    blocks, rows = args[2].shape[:2]
    K, E, H = args[8].shape
    fits = (
        blocks == 1 and args[0].shape[0] == 1 and args[0].shape[1] == rows and rows == S * 2 * ROWS
        and DP == 4 and S % DP == 0 and S // DP <= 16 and S <= 128
        and E == 128 and H == K * 64 and K == 2 * DP and 64 % (8 * S) == 0
    )
    return fused_body(*args) if fits else plain_body(*args)


def solution(mesh):
    placed = (
        P("dp", "seq", None),
        P("dp", "seq", None),
        P("seq", None, None),
        P(None, "seq", None),
        P(),
        P(),
        P(),
        P(),
        P(),
        P(),
        P(),
    )
    return jax.shard_map(
        body,
        mesh=mesh,
        in_specs=placed,
        out_specs=(
            P("dp", "seq", None),
            P("seq", None, "dp"),
            P(None, "seq", "dp"),
            P("dp", None, "seq"),
            P("dp", None, "seq"),
            P("dp", None, "seq"),
        ),
        check_vma=False,
    )
```

```python
import jax
import jax.numpy as jnp
from jax import lax
from jax.experimental import pallas as pl
from jax.experimental.pallas import tpu as pltpu
from jax.sharding import PartitionSpec as P

epsilon = 1e-05


def inverse_rms(values):
    return lax.rsqrt(jnp.mean(values * values, axis=-1, keepdims=True) + epsilon)


def norm_backward(grad_normed, normed_values, inverse):
    return inverse * (
        grad_normed - normed_values * jnp.mean(grad_normed * normed_values, axis=-1, keepdims=True)
    )


def plain_body(
    tokens,
    cotangent,
    first_factor,
    second_factor,
    norm_gain,
    gate_scale,
    gate_bias,
    mlp_gain,
    gate_weight,
    up_weight,
    down_weight,
):
    inputs = tokens[0]
    upstream = cotangent[0]
    rows_local, width = inputs.shape
    local_blocks, block_size = (first_factor.shape[0], first_factor.shape[1])
    mlp_blocks, block_in, block_hidden = gate_weight.shape
    inputs_wide = inputs.astype(jnp.float32)
    first_inverse = inverse_rms(inputs_wide)
    first_normed = inputs_wide * first_inverse
    normed_tokens = (first_normed * norm_gain).astype(jnp.bfloat16)
    blocked = normed_tokens.reshape(local_blocks, block_size, width)
    section_one = jnp.einsum(
        "bij,bjd->bid", first_factor, blocked, preferred_element_type=jnp.float32
    ).astype(jnp.bfloat16)
    section_cols = lax.all_to_all(section_one, "seq", split_axis=1, concat_axis=0, tiled=True)
    mixed_cols = jnp.einsum(
        "cib,bid->cid", second_factor, section_cols, preferred_element_type=jnp.float32
    ).astype(jnp.bfloat16)
    mixed_rows = lax.all_to_all(mixed_cols, "seq", split_axis=0, concat_axis=1, tiled=True).reshape(
        rows_local, width
    )
    mixed_wide = mixed_rows.astype(jnp.float32)
    gate_open = jax.nn.sigmoid(normed_tokens.astype(jnp.float32) * gate_scale + gate_bias)
    after_mix = (inputs_wide + mixed_wide * gate_open).astype(jnp.bfloat16)
    after_wide = after_mix.astype(jnp.float32)
    second_inverse = inverse_rms(after_wide)
    second_normed = after_wide * second_inverse
    mlp_input = (
        (second_normed * mlp_gain).astype(jnp.bfloat16).reshape(rows_local, mlp_blocks, block_in)
    )
    pre_gate = jnp.einsum(
        "tkd,kdh->tkh", mlp_input, gate_weight, preferred_element_type=jnp.float32
    )
    pre_up = jnp.einsum("tkd,kdh->tkh", mlp_input, up_weight, preferred_element_type=jnp.float32)
    sig_gate = jax.nn.sigmoid(pre_gate)
    hidden = (pre_gate * sig_gate * pre_up).astype(jnp.bfloat16)
    permuted = jnp.transpose(hidden, (0, 2, 1)).reshape(rows_local, mlp_blocks, block_hidden)
    upstream_wide = upstream.astype(jnp.float32)
    upstream_blocks = upstream.reshape(rows_local, mlp_blocks, block_in)
    grad_perm = jnp.einsum(
        "tkd,kdh->tkh", upstream_blocks, down_weight, preferred_element_type=jnp.float32
    ).astype(jnp.bfloat16)
    grad_hidden = jnp.transpose(
        grad_perm.reshape(rows_local, block_hidden, mlp_blocks), (0, 2, 1)
    ).astype(jnp.float32)
    grad_gate_pre = (grad_hidden * pre_up * sig_gate * (1.0 + pre_gate * (1.0 - sig_gate))).astype(
        jnp.bfloat16
    )
    grad_up_pre = (grad_hidden * pre_gate * sig_gate).astype(jnp.bfloat16)
    grad_inner = jnp.einsum(
        "tkh,kdh->tkd", grad_gate_pre, gate_weight, preferred_element_type=jnp.float32
    )
    grad_inner = grad_inner + jnp.einsum(
        "tkh,kdh->tkd", grad_up_pre, up_weight, preferred_element_type=jnp.float32
    )
    grad_inner = grad_inner.reshape(rows_local, width)
    grad_after = (
        upstream_wide + norm_backward(grad_inner * mlp_gain, second_normed, second_inverse)
    ).astype(jnp.bfloat16)
    grad_after_wide = grad_after.astype(jnp.float32)
    grad_mixed = (grad_after_wide * gate_open).astype(jnp.bfloat16)
    grad_open = grad_after_wide * mixed_wide * gate_open * (1.0 - gate_open)
    grad_mixed_cols = lax.all_to_all(
        grad_mixed.reshape(local_blocks, block_size, width),
        "seq",
        split_axis=1,
        concat_axis=0,
        tiled=True,
    )
    grad_section_cols = jnp.einsum(
        "cib,cid->bid", second_factor, grad_mixed_cols, preferred_element_type=jnp.float32
    ).astype(jnp.bfloat16)
    second_term = jnp.einsum(
        "cid,bid->cib", grad_mixed_cols, section_cols, preferred_element_type=jnp.float32
    )
    grad_section = lax.all_to_all(grad_section_cols, "seq", split_axis=0, concat_axis=1, tiled=True)
    first_term = jnp.einsum(
        "bid,bjd->bij", grad_section, blocked, preferred_element_type=jnp.float32
    )
    grad_normed = jnp.einsum(
        "bij,bid->bjd", first_factor, grad_section, preferred_element_type=jnp.float32
    ).reshape(rows_local, width)
    grad_normed = grad_normed + grad_open * gate_scale
    grad_inputs = (
        grad_after_wide + norm_backward(grad_normed * norm_gain, first_normed, first_inverse)
    ).astype(jnp.bfloat16)
    factor_first, factor_second = (
        lax.psum_scatter(
            first_term.astype(jnp.bfloat16), "dp", scatter_dimension=2, tiled=True
        ).astype(jnp.float32),
        lax.psum_scatter(
            second_term.astype(jnp.bfloat16), "dp", scatter_dimension=2, tiled=True
        ).astype(jnp.float32),
    )
    replicas = lax.axis_size("dp")
    factor_weight = (replicas * width) ** (-0.5)
    mlp_weight = (replicas * rows_local * lax.axis_size("seq")) ** (-0.5)
    gate_term = jnp.einsum(
        "tkd,tkh->kdh", mlp_input, grad_gate_pre, preferred_element_type=jnp.float32
    )
    up_term = jnp.einsum("tkd,tkh->kdh", mlp_input, grad_up_pre, preferred_element_type=jnp.float32)
    down_term = jnp.einsum(
        "tkd,tkh->kdh", upstream_blocks, permuted, preferred_element_type=jnp.float32
    )
    stacked = jnp.concatenate([gate_term, up_term, down_term], axis=1)
    seq_summed = lax.psum_scatter(stacked, "seq", scatter_dimension=2, tiled=True)
    reduced = lax.psum_scatter(seq_summed, "dp", scatter_dimension=0, tiled=True)
    reduced = reduced * mlp_weight
    grad_gate = reduced[:, 0:block_in, :]
    grad_up = reduced[:, block_in : 2 * block_in, :]
    grad_down = reduced[:, 2 * block_in : 3 * block_in, :]
    return (
        grad_inputs[None],
        factor_first * factor_weight,
        factor_second * factor_weight,
        grad_gate,
        grad_up,
        grad_down,
    )


MESH = pl.DeviceIdType.MESH
F32 = jnp.float32
BF16 = jnp.bfloat16
ROWS = 16
UNR = 8


def mm(a, b, da=1, db=0):
    return lax.dot_general(a, b, (((da,), (db,)), ((), ())), preferred_element_type=F32)


def mult(v, m):
    return v if isinstance(v, int) else pl.multiple_of(v, m)


def row_loop(total, step, fn):
    def one(n, carry):
        fn(pl.ds(mult(n * step, step), step))
        return carry

    lax.fori_loop(0, total // step, one, 0, unroll=UNR)


def count_loop(total, fn):
    def one(n, carry):
        fn(n)
        return carry

    lax.fori_loop(0, total, one, 0)


def fused(
    S, DP,
    tok, cot_in, ff, sf, gain1, scale1, bias1, gain2, gw_in, uw_in, dw_in,
    gtok, facs, wout,
    normed, sec_out, sec_cols, mc_out, mixed, opened, gm_out, gm_cols, gs_out, gs,
    mix, mix_t, onehot, w2, gh, hid, gg, gu, inner, norm2, inv2s, ginner, gos, gres,
    cot, gw, uw, dw, cotp, ffp, ws, rc, xo, rx, yo, ry, lo, rl, ho, rh, ft, rf,
    send, recv, csend, crecv, xsend, xrecv, ysend, yrecv, losend, lorecv, hisend, hirecv, fsend, frecv, lsem,
):
    me = lax.axis_index("seq")
    dp = lax.axis_index("dp")
    core = lax.rem(dp, 2)
    peer_core = dp + 1 - 2 * core
    peer_x = lax.rem(dp + 2, DP)
    rows, width = tok.shape
    K, E, H = gw.shape
    chunk = H // K
    ic = rows // S
    hs = H // S
    nbd = S // DP
    kd = K // DP
    half = rows // 2
    part = ic // 2
    ZS = S // 2
    yy = lax.rem(me, 2)
    lo_z = lax.rem(lax.div(me, 2), 2)
    hi_z = lax.div(me, 4)

    loads = []
    for n, (a, b) in enumerate(((cot_in, cot), (dw_in, dw), (gw_in, gw), (uw_in, uw))):
        load = pltpu.make_async_copy(a, b, lsem.at[n])
        load.start()
        loads.append(load)
    barrier = pltpu.get_barrier_semaphore()
    for r in range(1, S):
        pl.semaphore_signal(barrier, inc=1, device_id={"seq": lax.rem(me + r, S)}, device_id_type=MESH)
    for r in range(1, DP):
        pl.semaphore_signal(barrier, inc=1, device_id={"dp": lax.rem(dp + r, DP)}, device_id_type=MESH)

    def first_norm(s):
        v = tok[s, :].astype(F32)
        inv = lax.rsqrt(jnp.mean(v * v, axis=-1, keepdims=True) + epsilon)
        normed[s, :] = (v * inv * gain1[...]).astype(BF16)

    row_loop(rows, ROWS, first_norm)
    for q in range(S):
        for h in range(2):
            ffp[h * half + q * part : h * half + (q + 1) * part, :] = ff[q * ic + h * part : q * ic + (h + 1) * part, :]

    def aligned(start):
        return pl.ds(mult(start, part), part)

    def exchange(phase, h, src, dst):
        def where(ref, q):
            return ref.at[h, aligned(q * part)]

        copies = []
        for r in range(1, S):
            q = lax.rem(me + r, S)
            cp = pltpu.make_async_remote_copy(
                src_ref=where(src, q),
                dst_ref=where(dst, me),
                send_sem=send.at[phase, h, r],
                recv_sem=recv.at[phase, h, r],
                device_id={"seq": q},
                device_id_type=MESH,
            )
            cp.start()
            copies.append(cp)
        where(dst, me)[...] = where(src, me)[...]
        return copies

    pending = []
    one = []
    for h in range(2):
        sec_out[h] = mm(ffp[h * half : (h + 1) * half, :], normed[...]).astype(BF16)
        if h == 0:
            pl.semaphore_wait(barrier, S - 1 + DP - 1)
        one.append(exchange(0, h, sec_out, sec_cols))
    pending += one[0] + one[1]

    def open_gate(s):
        opened[s, :] = jax.nn.sigmoid(normed[s, :].astype(F32) * scale1[...] + bias1[...])

    row_loop(rows, ROWS, open_gate)
    ri = lax.broadcasted_iota(jnp.int32, (half, half), 0)
    ci = lax.broadcasted_iota(jnp.int32, (half, half), 1)
    same = lax.rem(ri, part) == lax.rem(ci, part)
    er = lax.broadcasted_iota(jnp.int32, (half, S), 0)
    ec = lax.broadcasted_iota(jnp.int32, (half, S), 1)
    expand = jnp.where(lax.div(er, part) == ec, 1.0, 0.0).astype(BF16)
    pi = lax.broadcasted_iota(jnp.int32, (part, half), 0)
    pj = lax.rem(lax.broadcasted_iota(jnp.int32, (part, half), 1), part)
    for c in range(S):
        spread_c = mm(sf[c], expand, 0, 1)
        for h in range(2):
            rows_c = jnp.where(pi == pj, spread_c[h * part : (h + 1) * part, :], 0.0)
            mix[h, c * part : (c + 1) * part, :] = rows_c.astype(BF16)
    for h in range(2):
        mix_t[h] = jnp.transpose(mix[h].astype(F32)).astype(BF16)

    def regroup(n):
        for h in range(2):
            cotp[aligned(h * half + n * part), :] = cot[aligned(n * ic + h * part), :]

    loads[0].wait()
    count_loop(S, regroup)

    def hot_rows(s):
        hi = lax.broadcasted_iota(jnp.int32, (ROWS, K * 128), 0) + s.start
        hc = lax.broadcasted_iota(jnp.int32, (ROWS, K * 128), 1)
        lane = lax.rem(hc, 128)
        hit = hi == lax.rem(lane, chunk) * K + lax.div(hc, 128)
        for r in range(2):
            onehot[r, s, :] = jnp.where(hit & (lax.div(lane, chunk) == r), 1.0, 0.0).astype(BF16)

    row_loop(H, ROWS, hot_rows)

    def spread(p):
        for r in range(2):
            w2[p, r * E : (r + 1) * E, :] = mm(dw[2 * p + r], onehot[r]).astype(BF16)

    loads[1].wait()
    for p in range(K // 2):
        spread(p)
    two = []
    for h in range(2):
        for cp in one[h]:
            cp.wait_recv()
        mc_out[h] = mm(mix[h], sec_cols[h]).astype(BF16)
        two.append(exchange(1, h, mc_out, mixed))
    pending += two[0] + two[1]

    def hidden_grad(p):
        g = mm(cotp[:, pl.ds(mult(p * 2 * E, 2 * E), 2 * E)], w2[p]).astype(BF16)
        for k in range(K):
            gh[k, :, pl.ds(mult(p * 128, 128), 128)] = g[:, k * 128 : (k + 1) * 128]

    for p in range(K // 2):
        hidden_grad(p)
    def second_norm(h, n):
        nat, own = aligned(n * ic + h * part), aligned(n * part)
        s = aligned(h * half + n * part)
        resid = (tok[nat, :].astype(F32) + mixed[h, own, :].astype(F32) * opened[nat, :]).astype(BF16).astype(F32)
        inv = lax.rsqrt(jnp.mean(resid * resid, axis=-1, keepdims=True) + epsilon)
        n2 = resid * inv
        norm2[s, :] = n2
        inv2s[s, :] = jnp.broadcast_to(inv, (part, 128))
        inner[s, :] = (n2 * gain2[...]).astype(BF16)

    def mlp(h, k):
        cols = slice(k * E, k * E + E)
        mine = slice(h * half, (h + 1) * half)
        x = inner[mine, cols]
        for c0 in range(0, H, 256):
            cs = slice(c0, c0 + 256)
            va = mm(x, gw[k, :, cs])
            vu = mm(x, uw[k, :, cs])
            for n in range(0, half, 16):
                a, u = va[n : n + 16], vu[n : n + 16]
                t = slice(h * half + n, h * half + n + 16)
                g = gh[k, t, cs].astype(F32)
                sig = 0.5 * jnp.tanh(0.5 * a) + 0.5
                silu = a * sig
                hid[k, t, cs] = (silu * u).astype(BF16)
                gg[k, t, cs] = (g * u * (sig + silu * (1.0 - sig))).astype(BF16)
                gu[k, t, cs] = (g * silu).astype(BF16)
        ginner[mine, cols] = mm(gg[k, mine, :], gw[k], 1, 1) + mm(gu[k, mine, :], uw[k], 1, 1)

    def second_back(h, n):
        nat, own = aligned(n * ic + h * part), aligned(n * part)
        s = aligned(h * half + n * part)
        n2 = norm2[s, :]
        dn = ginner[s, :] * gain2[...]
        mean = jnp.mean(dn * n2, axis=-1, keepdims=True)
        gr = (cot[nat, :].astype(F32) + inv2s[s, 0:1] * (dn - n2 * mean)).astype(BF16)
        gres[nat, :] = gr
        wide = gr.astype(F32)
        op = opened[nat, :]
        gm_out[h, own, :] = (wide * op).astype(BF16)
        gos[nat, :] = wide * mixed[h, own, :].astype(F32) * op * (1.0 - op) * scale1[...]

    loads[2].wait()
    loads[3].wait()
    three = []
    for h in range(2):
        for cp in two[h]:
            cp.wait_recv()
        for n in range(S):
            second_norm(h, n)
        for k in range(K):
            mlp(h, k)
        for n in range(S):
            second_back(h, n)
        three.append(exchange(2, h, gm_out, gm_cols))
    pending += three[0] + three[1]

    share = rows // DP
    pr = lax.broadcasted_iota(jnp.int32, (DP * 16, half), 0)
    pc = lax.div(lax.broadcasted_iota(jnp.int32, (DP * 16, half), 1), part)
    pick = (lax.div(pr, 16) == lax.div(pc, nbd)) & (lax.rem(pr, 16) == lax.rem(pc, nbd))
    pick = jnp.where(pick, 1.0, 0.0).astype(BF16)
    four = [None, None]

    def back_mix(h):
        for cp in three[h]:
            cp.wait_recv()
        gs_out[h] = mm(mix_t[h], gm_cols[h]).astype(BF16)
        four[h] = exchange(3, h, gs_out, gs)
        pending.extend(four[h])

    def outer(h):
        both = jnp.where(same, mm(sec_cols[h], gm_cols[h], 1, 1), 0.0).astype(BF16)
        picked = mm(pick, both).astype(BF16)
        for d in range(DP):
            ft[h, d, share : share + 16, :] = picked[d * 16 : (d + 1) * 16, :]

    arrivals = {}

    def start(key, src, dst, send_sem, recv_sem, device):
        cp = pltpu.make_async_remote_copy(
            src_ref=src, dst_ref=dst, send_sem=send_sem, recv_sem=recv_sem, device_id=device, device_id_type=MESH
        )
        cp.start()
        arrivals[key] = cp
        pending.append(cp)

    far_mine = lax.rem(dp + 2, DP)
    far_peer = lax.rem(peer_core + 2, DP)

    def spot(q):
        return (q % 2) * 4 + (q // 2) % 2 * 2 + q // 4

    def down_term(p):
        for r in range(2):
            c = cotp[:, (2 * p + r) * E : (2 * p + r + 1) * E]
            parts = []
            for k in range(K):
                raw = mm(hid[k, :, p * 128 : (p + 1) * 128], c, 0, 0)
                parts.append(raw[r * chunk : (r + 1) * chunk, :])
            size = chunk // S
            for q in range(S):
                piece = jnp.concatenate([v[q * size : (q + 1) * size, :] for v in parts], axis=0)
                ws[0, r, p, spot(q)] = piece.astype(BF16)

    def in_term(j, grads, p):
        for r in range(2):
            x = inner[:, (2 * p + r) * E : (2 * p + r + 1) * E]
            raw = mm(grads[2 * p + r], x, 0, 0).astype(BF16)
            for q in range(S):
                ws[j, r, p, spot(q)] = raw[q * hs : (q + 1) * hs, :]

    def terms(j):
        for p in range(K // 2):
            if j == 0:
                down_term(p)
            else:
                in_term(j, (gg, gu)[j - 1], p)
        for r in range(2):
            for slot, owner in enumerate((far_peer, peer_core)):
                start(
                    ("c", j, r, slot), ws.at[j, r, owner], rc.at[j, r, slot],
                    csend.at[j, r, slot], crecv.at[j, r, slot], {"dp": peer_core},
                )

    def over_x(j, r):
        arrivals["c", j, r, 0].wait_recv()
        for q in range(S):
            xo[j, r, q] = (ws[j, r, far_mine, q].astype(F32) + rc[j, r, 0, q].astype(F32)).astype(BF16)
        start(("x", j, r), xo.at[j, r], rx.at[j, r], xsend.at[j, r], xrecv.at[j, r], {"dp": peer_x})

    def partial(j, r, q):
        return ws[j, r, dp, q].astype(F32) + rc[j, r, 1, q].astype(F32) + rx[j, r, q].astype(F32)

    def over_y(j, r):
        arrivals["c", j, r, 1].wait_recv()
        arrivals["x", j, r].wait_recv()
        for z in range(4):
            yo[j, r, z] = partial(j, r, (1 - yy) * 4 + z).astype(BF16)
        start(("y", j, r), yo.at[j, r], ry.at[j, r], ysend.at[j, r], yrecv.at[j, r], {"seq": me + 1 - 2 * yy})

    def after_y(j, r, z):
        return partial(j, r, yy * 4 + z) + ry[j, r, z].astype(F32)

    def over_lo(j, r):
        arrivals["y", j, r].wait_recv()
        for z in range(2):
            lo[j, r, z] = after_y(j, r, (1 - lo_z) * 2 + z).astype(BF16)
        start(("l", j, r), lo.at[j, r], rl.at[j, r], losend.at[j, r], lorecv.at[j, r], {"seq": me + 2 - 4 * lo_z})

    def after_lo(j, r, z):
        return after_y(j, r, lo_z * 2 + z) + rl[j, r, z].astype(F32)

    def over_hi(j, r):
        arrivals["l", j, r].wait_recv()
        ho[j, r] = after_lo(j, r, 1 - hi_z).astype(BF16)
        start(("h", j, r), ho.at[j, r], rh.at[j, r], hisend.at[j, r], hirecv.at[j, r], {"seq": me + 4 - 8 * hi_z})

    def finish(j, r):
        arrivals["h", j, r].wait_recv()
        scale = (DP * rows * S) ** (-0.5)
        wout[j, r * hs : (r + 1) * hs, :] = (after_lo(j, r, hi_z) + rh[j, r].astype(F32)) * scale

    def factor(h):
        for cp in four[h]:
            cp.wait_recv()
        f1 = mm(normed[...], gs[h], 1, 1).astype(BF16)
        for d in range(DP):
            ft[h, d, 0:share, :] = f1[d * share : (d + 1) * share, :]
        for r in range(1, DP):
            d = lax.rem(dp + r, DP)
            start(("f", h, r), ft.at[h, d], rf.at[h, r], fsend.at[h, r], frecv.at[h, r], {"dp": d})

    def first_back(s):
        v = tok[s, :].astype(F32)
        inv = lax.rsqrt(jnp.mean(v * v, axis=-1, keepdims=True) + epsilon)
        n1 = v * inv
        dm = (ginner[s, :] + gos[s, :]) * gain1[...]
        mean = jnp.mean(dm * n1, axis=-1, keepdims=True)
        gtok[s, :] = (gres[s, :].astype(F32) + inv * (dm - n1 * mean)).astype(BF16)

    def token_grad():
        ginner[...] = mm(ffp[...], gs[...].reshape(rows, width), 0, 0)
        row_loop(rows, ROWS, first_back)

    def factor_sum(h):
        for r in range(1, DP):
            arrivals["f", h, r].wait_recv()
        total = ft[h, dp].astype(F32)
        for r in range(1, DP):
            total = total + rf[h, r].astype(F32)
        facs[:, h * half : (h + 1) * half] = total * ((DP * width) ** (-0.5))

    terms(1)
    terms(2)
    over_x(1, 0)
    over_x(1, 1)
    terms(0)
    over_x(2, 0)
    over_x(2, 1)
    back_mix(0)
    over_x(0, 0)
    over_x(0, 1)
    outer(0)
    back_mix(1)
    outer(1)
    over_y(1, 0)
    over_y(1, 1)
    over_y(2, 0)
    over_y(2, 1)
    factor(0)
    over_y(0, 0)
    over_y(0, 1)
    factor(1)
    over_lo(1, 0)
    over_lo(1, 1)
    over_lo(2, 0)
    over_lo(2, 1)
    over_lo(0, 0)
    over_lo(0, 1)
    token_grad()
    over_hi(1, 0)
    over_hi(1, 1)
    over_hi(2, 0)
    over_hi(2, 1)
    over_hi(0, 0)
    over_hi(0, 1)
    factor_sum(0)
    factor_sum(1)
    finish(1, 0)
    finish(1, 1)
    finish(2, 0)
    finish(2, 1)
    finish(0, 0)
    finish(0, 1)
    for cp in pending:
        cp.wait_send()


def arrange(S, share, part, kd, step, gtok_in, facs, wout, gtok, first, second, gate, up, down):
    gtok[...] = gtok_in[...]
    nbd = second.shape[1]
    half = S * part
    pieces = [facs[0:share, h * half + q * part : h * half + (q + 1) * part] for q in range(S) for h in range(2)]
    first[...] = jnp.concatenate(pieces, axis=1)
    for c in range(S):
        pieces = [facs[share : share + nbd, h * half + c * part : h * half + (c + 1) * part] for h in range(2)]
        second[c] = jnp.concatenate(pieces, axis=1)
    gate[...] = wout[1]
    up[...] = wout[2]
    size = wout.shape[1] // kd
    K = size // step
    for d in range(kd):
        for k in range(K):
            at = d * size + k * step
            down[pl.ds(d * size + k, step, stride=K), :] = wout[0, at : at + step, :]


def fused_body(
    tokens, cotangent, first_factor, second_factor, norm_gain, gate_scale, gate_bias, mlp_gain,
    gate_weight, up_weight, down_weight,
):
    S, DP = lax.axis_size("seq"), lax.axis_size("dp")
    rows, width = tokens.shape[1:]
    K, E, H = gate_weight.shape
    ic = rows // S
    nbd = S // DP
    hs = H // S
    kd = K // DP
    share = rows // DP
    part = ic // 2
    split = jnp.transpose(second_factor, (0, 2, 1))
    gains = [v.reshape(1, width) for v in (norm_gain, gate_scale, gate_bias, mlp_gain)]
    full = (rows, width)
    vm = pltpu.VMEM
    owned = vm((3, 2, S, hs, E), BF16)
    wide = vm(full, F32)
    half = vm(full, BF16)
    pair = vm((2, rows // 2, width), BF16)
    deep = vm((K, rows, H), BF16)
    dma = pltpu.SemaphoreType.DMA
    scratch = [
        half, pair, pair, pair, pair, wide, pair, pair, pair, pair,
        vm((2, rows // 2, rows // 2), BF16), vm((2, rows // 2, rows // 2), BF16), vm((2, H, K * 128), BF16),
        vm((K // 2, 2 * E, K * 128), BF16), deep, deep, deep, deep,
        half, wide, vm((rows, 128), F32), wide, wide, half,
        half, vm((K, E, H), BF16), vm((K, E, H), BF16), vm((K, E, H), BF16),
        half, vm((rows, rows), BF16), vm((3, 2, DP, S, hs, E), BF16), vm((3, 2, 2, S, hs, E), BF16), owned, owned,
        vm((3, 2, 4, hs, E), BF16), vm((3, 2, 4, hs, E), BF16), vm((3, 2, 2, hs, E), BF16), vm((3, 2, 2, hs, E), BF16),
        vm((3, 2, hs, E), BF16), vm((3, 2, hs, E), BF16),
        vm((2, DP, share + 16, rows // 2), BF16), vm((2, DP, share + 16, rows // 2), BF16),
        dma((4, 2, S)), dma((4, 2, S)), dma((3, 2, 2)), dma((3, 2, 2)), dma((3, 2)), dma((3, 2)),
        dma((3, 2)), dma((3, 2)), dma((3, 2)), dma((3, 2)), dma((3, 2)), dma((3, 2)), dma((2, DP)), dma((2, DP)), dma((4,)),
    ]
    whole = pl.BlockSpec(memory_space=pltpu.VMEM)
    away = pl.BlockSpec(memory_space=pl.ANY)
    gtok, facs, wout = pl.pallas_call(
        lambda *refs: fused(S, DP, *refs),
        out_shape=(
            jax.ShapeDtypeStruct(full, BF16),
            jax.ShapeDtypeStruct((share + 16, rows), F32),
            jax.ShapeDtypeStruct((3, kd * hs, E), F32),
        ),
        in_specs=[whole, away] + [whole] * 6 + [away] * 3,
        out_specs=(whole,) * 3,
        scratch_shapes=scratch,
        compiler_params=pltpu.CompilerParams(
            collective_id=0, has_side_effects=True, vmem_limit_bytes=62 * 1024 * 1024
        ),
    )(tokens[0], cotangent[0], first_factor[0], split, *gains, gate_weight, up_weight, down_weight)
    outs = pl.pallas_call(
        lambda *refs: arrange(S, share, part, kd, hs // K, *refs),
        out_shape=(
            jax.ShapeDtypeStruct(full, BF16),
            jax.ShapeDtypeStruct((share, rows), F32),
            jax.ShapeDtypeStruct((S, nbd, ic), F32),
            jax.ShapeDtypeStruct((kd * hs, E), F32),
            jax.ShapeDtypeStruct((kd * hs, E), F32),
            jax.ShapeDtypeStruct((kd * hs, E), F32),
        ),
        in_specs=[whole] * 3,
        out_specs=(whole,) * 6,
    )(gtok, facs, wout)
    gtok, first, second, gate, up, down = outs
    gate, up, down = [jnp.transpose(w.reshape(kd, hs, E), (0, 2, 1)) for w in (gate, up, down)]
    return gtok[None], first.T[None], jnp.transpose(second, (0, 2, 1)), gate, up, down


def body(*args):
    S, DP = lax.axis_size("seq"), lax.axis_size("dp")
    blocks, rows = args[2].shape[:2]
    K, E, H = args[8].shape
    fits = (
        S == 8 and blocks == 1 and args[0].shape[0] == 1 and args[0].shape[1] == rows and rows == S * 2 * ROWS
        and DP == 4 and S % DP == 0 and S // DP <= 16 and S <= 128
        and E == 128 and H == K * 64 and K == 2 * DP and 64 % (8 * S) == 0
    )
    return fused_body(*args) if fits else plain_body(*args)


def solution(mesh):
    placed = (
        P("dp", "seq", None),
        P("dp", "seq", None),
        P("seq", None, None),
        P(None, "seq", None),
        P(),
        P(),
        P(),
        P(),
        P(),
        P(),
        P(),
    )
    return jax.shard_map(
        body,
        mesh=mesh,
        in_specs=placed,
        out_specs=(
            P("dp", "seq", None),
            P("seq", None, "dp"),
            P(None, "seq", "dp"),
            P("dp", None, "seq"),
            P("dp", None, "seq"),
            P("dp", None, "seq"),
        ),
        check_vma=False,
    )
```

```python
import jax
import jax.numpy as jnp
from jax import lax
from jax.experimental import pallas as pl
from jax.experimental.pallas import tpu as pltpu
from jax.sharding import PartitionSpec as P

epsilon = 1e-05


def inverse_rms(values):
    return lax.rsqrt(jnp.mean(values * values, axis=-1, keepdims=True) + epsilon)


def norm_backward(grad_normed, normed_values, inverse):
    return inverse * (
        grad_normed - normed_values * jnp.mean(grad_normed * normed_values, axis=-1, keepdims=True)
    )


def plain_body(
    tokens,
    cotangent,
    first_factor,
    second_factor,
    norm_gain,
    gate_scale,
    gate_bias,
    mlp_gain,
    gate_weight,
    up_weight,
    down_weight,
):
    inputs = tokens[0]
    upstream = cotangent[0]
    rows_local, width = inputs.shape
    local_blocks, block_size = (first_factor.shape[0], first_factor.shape[1])
    mlp_blocks, block_in, block_hidden = gate_weight.shape
    inputs_wide = inputs.astype(jnp.float32)
    first_inverse = inverse_rms(inputs_wide)
    first_normed = inputs_wide * first_inverse
    normed_tokens = (first_normed * norm_gain).astype(jnp.bfloat16)
    blocked = normed_tokens.reshape(local_blocks, block_size, width)
    section_one = jnp.einsum(
        "bij,bjd->bid", first_factor, blocked, preferred_element_type=jnp.float32
    ).astype(jnp.bfloat16)
    section_cols = lax.all_to_all(section_one, "seq", split_axis=1, concat_axis=0, tiled=True)
    mixed_cols = jnp.einsum(
        "cib,bid->cid", second_factor, section_cols, preferred_element_type=jnp.float32
    ).astype(jnp.bfloat16)
    mixed_rows = lax.all_to_all(mixed_cols, "seq", split_axis=0, concat_axis=1, tiled=True).reshape(
        rows_local, width
    )
    mixed_wide = mixed_rows.astype(jnp.float32)
    gate_open = jax.nn.sigmoid(normed_tokens.astype(jnp.float32) * gate_scale + gate_bias)
    after_mix = (inputs_wide + mixed_wide * gate_open).astype(jnp.bfloat16)
    after_wide = after_mix.astype(jnp.float32)
    second_inverse = inverse_rms(after_wide)
    second_normed = after_wide * second_inverse
    mlp_input = (
        (second_normed * mlp_gain).astype(jnp.bfloat16).reshape(rows_local, mlp_blocks, block_in)
    )
    pre_gate = jnp.einsum(
        "tkd,kdh->tkh", mlp_input, gate_weight, preferred_element_type=jnp.float32
    )
    pre_up = jnp.einsum("tkd,kdh->tkh", mlp_input, up_weight, preferred_element_type=jnp.float32)
    sig_gate = jax.nn.sigmoid(pre_gate)
    hidden = (pre_gate * sig_gate * pre_up).astype(jnp.bfloat16)
    permuted = jnp.transpose(hidden, (0, 2, 1)).reshape(rows_local, mlp_blocks, block_hidden)
    upstream_wide = upstream.astype(jnp.float32)
    upstream_blocks = upstream.reshape(rows_local, mlp_blocks, block_in)
    grad_perm = jnp.einsum(
        "tkd,kdh->tkh", upstream_blocks, down_weight, preferred_element_type=jnp.float32
    ).astype(jnp.bfloat16)
    grad_hidden = jnp.transpose(
        grad_perm.reshape(rows_local, block_hidden, mlp_blocks), (0, 2, 1)
    ).astype(jnp.float32)
    grad_gate_pre = (grad_hidden * pre_up * sig_gate * (1.0 + pre_gate * (1.0 - sig_gate))).astype(
        jnp.bfloat16
    )
    grad_up_pre = (grad_hidden * pre_gate * sig_gate).astype(jnp.bfloat16)
    grad_inner = jnp.einsum(
        "tkh,kdh->tkd", grad_gate_pre, gate_weight, preferred_element_type=jnp.float32
    )
    grad_inner = grad_inner + jnp.einsum(
        "tkh,kdh->tkd", grad_up_pre, up_weight, preferred_element_type=jnp.float32
    )
    grad_inner = grad_inner.reshape(rows_local, width)
    grad_after = (
        upstream_wide + norm_backward(grad_inner * mlp_gain, second_normed, second_inverse)
    ).astype(jnp.bfloat16)
    grad_after_wide = grad_after.astype(jnp.float32)
    grad_mixed = (grad_after_wide * gate_open).astype(jnp.bfloat16)
    grad_open = grad_after_wide * mixed_wide * gate_open * (1.0 - gate_open)
    grad_mixed_cols = lax.all_to_all(
        grad_mixed.reshape(local_blocks, block_size, width),
        "seq",
        split_axis=1,
        concat_axis=0,
        tiled=True,
    )
    grad_section_cols = jnp.einsum(
        "cib,cid->bid", second_factor, grad_mixed_cols, preferred_element_type=jnp.float32
    ).astype(jnp.bfloat16)
    second_term = jnp.einsum(
        "cid,bid->cib", grad_mixed_cols, section_cols, preferred_element_type=jnp.float32
    )
    grad_section = lax.all_to_all(grad_section_cols, "seq", split_axis=0, concat_axis=1, tiled=True)
    first_term = jnp.einsum(
        "bid,bjd->bij", grad_section, blocked, preferred_element_type=jnp.float32
    )
    grad_normed = jnp.einsum(
        "bij,bid->bjd", first_factor, grad_section, preferred_element_type=jnp.float32
    ).reshape(rows_local, width)
    grad_normed = grad_normed + grad_open * gate_scale
    grad_inputs = (
        grad_after_wide + norm_backward(grad_normed * norm_gain, first_normed, first_inverse)
    ).astype(jnp.bfloat16)
    factor_first, factor_second = (
        lax.psum_scatter(
            first_term.astype(jnp.bfloat16), "dp", scatter_dimension=2, tiled=True
        ).astype(jnp.float32),
        lax.psum_scatter(
            second_term.astype(jnp.bfloat16), "dp", scatter_dimension=2, tiled=True
        ).astype(jnp.float32),
    )
    replicas = lax.axis_size("dp")
    factor_weight = (replicas * width) ** (-0.5)
    mlp_weight = (replicas * rows_local * lax.axis_size("seq")) ** (-0.5)
    gate_term = jnp.einsum(
        "tkd,tkh->kdh", mlp_input, grad_gate_pre, preferred_element_type=jnp.float32
    )
    up_term = jnp.einsum("tkd,tkh->kdh", mlp_input, grad_up_pre, preferred_element_type=jnp.float32)
    down_term = jnp.einsum(
        "tkd,tkh->kdh", upstream_blocks, permuted, preferred_element_type=jnp.float32
    )
    stacked = jnp.concatenate([gate_term, up_term, down_term], axis=1)
    seq_summed = lax.psum_scatter(stacked, "seq", scatter_dimension=2, tiled=True)
    reduced = lax.psum_scatter(seq_summed, "dp", scatter_dimension=0, tiled=True)
    reduced = reduced * mlp_weight
    grad_gate = reduced[:, 0:block_in, :]
    grad_up = reduced[:, block_in : 2 * block_in, :]
    grad_down = reduced[:, 2 * block_in : 3 * block_in, :]
    return (
        grad_inputs[None],
        factor_first * factor_weight,
        factor_second * factor_weight,
        grad_gate,
        grad_up,
        grad_down,
    )


MESH = pl.DeviceIdType.MESH
F32 = jnp.float32
BF16 = jnp.bfloat16
ROWS = 16
UNR = 8


def mm(a, b, da=1, db=0):
    return lax.dot_general(a, b, (((da,), (db,)), ((), ())), preferred_element_type=F32)


def mult(v, m):
    return v if isinstance(v, int) else pl.multiple_of(v, m)


def row_loop(total, step, fn):
    def one(n, carry):
        fn(pl.ds(mult(n * step, step), step))
        return carry

    lax.fori_loop(0, total // step, one, 0, unroll=UNR)


def count_loop(total, fn):
    def one(n, carry):
        fn(n)
        return carry

    lax.fori_loop(0, total, one, 0)


def fused(
    S, DP,
    tok, cot_in, ff, sf, gain1, scale1, bias1, gain2, gw_in, uw_in, dw_in,
    gtok, facs, wout,
    normed, sec_out, sec_cols, mc_out, mixed, opened, gm_out, gm_cols, gs_out, gs,
    mix, mix_t, onehot, w2, gh, hid, gg, gu, inner, norm2, inv2s, ginner, gos, gres,
    cot, gw, uw, dw, cotp, ffp, ws, rc, xo, rx, yo, ry, xo2, rx2, yo2, ry2, zo, rz, lo, rl, ho, rh, ft, rf,
    send, recv, csend, crecv, xsend, xrecv, ysend, yrecv, losend, lorecv, hisend, hirecv, fsend, frecv, zsend, zrecv, lsem,
):
    me = lax.axis_index("seq")
    dp = lax.axis_index("dp")
    core = lax.rem(dp, 2)
    peer_core = dp + 1 - 2 * core
    peer_x = lax.rem(dp + 2, DP)
    rows, width = tok.shape
    K, E, H = gw.shape
    chunk = H // K
    ic = rows // S
    hs = H // S
    nbd = S // DP
    kd = K // DP
    half = rows // 2
    part = ic // 2
    ZS = S // 2
    yy = lax.rem(me, 2)
    lo_z = lax.rem(lax.div(me, 2), 2)
    hi_z = lax.div(me, 4)

    loads = []
    for n, (a, b) in enumerate(((cot_in, cot), (dw_in, dw), (gw_in, gw), (uw_in, uw))):
        load = pltpu.make_async_copy(a, b, lsem.at[n])
        load.start()
        loads.append(load)
    barrier = pltpu.get_barrier_semaphore()
    for r in range(1, S):
        pl.semaphore_signal(barrier, inc=1, device_id={"seq": lax.rem(me + r, S)}, device_id_type=MESH)
    for r in range(1, DP):
        pl.semaphore_signal(barrier, inc=1, device_id={"dp": lax.rem(dp + r, DP)}, device_id_type=MESH)

    def first_norm(s):
        v = tok[s, :].astype(F32)
        inv = lax.rsqrt(jnp.mean(v * v, axis=-1, keepdims=True) + epsilon)
        normed[s, :] = (v * inv * gain1[...]).astype(BF16)

    row_loop(rows, ROWS, first_norm)
    for q in range(S):
        for h in range(2):
            ffp[h * half + q * part : h * half + (q + 1) * part, :] = ff[q * ic + h * part : q * ic + (h + 1) * part, :]

    def aligned(start):
        return pl.ds(mult(start, part), part)

    def exchange(phase, h, src, dst):
        def where(ref, q):
            return ref.at[h, aligned(q * part)]

        copies = []
        for r in range(1, S):
            q = lax.rem(me + r, S)
            cp = pltpu.make_async_remote_copy(
                src_ref=where(src, q),
                dst_ref=where(dst, me),
                send_sem=send.at[phase, h, r],
                recv_sem=recv.at[phase, h, r],
                device_id={"seq": q},
                device_id_type=MESH,
            )
            cp.start()
            copies.append(cp)
        where(dst, me)[...] = where(src, me)[...]
        return copies

    pending = []
    one = []
    for h in range(2):
        sec_out[h] = mm(ffp[h * half : (h + 1) * half, :], normed[...]).astype(BF16)
        if h == 0:
            pl.semaphore_wait(barrier, S - 1 + DP - 1)
        one.append(exchange(0, h, sec_out, sec_cols))
    pending += one[0] + one[1]

    def open_gate(s):
        opened[s, :] = jax.nn.sigmoid(normed[s, :].astype(F32) * scale1[...] + bias1[...])

    row_loop(rows, ROWS, open_gate)
    ri = lax.broadcasted_iota(jnp.int32, (half, half), 0)
    ci = lax.broadcasted_iota(jnp.int32, (half, half), 1)
    same = lax.rem(ri, part) == lax.rem(ci, part)
    er = lax.broadcasted_iota(jnp.int32, (half, S), 0)
    ec = lax.broadcasted_iota(jnp.int32, (half, S), 1)
    expand = jnp.where(lax.div(er, part) == ec, 1.0, 0.0).astype(BF16)
    pi = lax.broadcasted_iota(jnp.int32, (part, half), 0)
    pj = lax.rem(lax.broadcasted_iota(jnp.int32, (part, half), 1), part)
    for c in range(S):
        spread_c = mm(sf[c], expand, 0, 1)
        for h in range(2):
            rows_c = jnp.where(pi == pj, spread_c[h * part : (h + 1) * part, :], 0.0)
            mix[h, c * part : (c + 1) * part, :] = rows_c.astype(BF16)
    for h in range(2):
        mix_t[h] = jnp.transpose(mix[h].astype(F32)).astype(BF16)

    def regroup(n):
        for h in range(2):
            cotp[aligned(h * half + n * part), :] = cot[aligned(n * ic + h * part), :]

    loads[0].wait()
    count_loop(S, regroup)

    def hot_rows(s):
        hi = lax.broadcasted_iota(jnp.int32, (ROWS, K * 128), 0) + s.start
        hc = lax.broadcasted_iota(jnp.int32, (ROWS, K * 128), 1)
        lane = lax.rem(hc, 128)
        hit = hi == lax.rem(lane, chunk) * K + lax.div(hc, 128)
        for r in range(2):
            onehot[r, s, :] = jnp.where(hit & (lax.div(lane, chunk) == r), 1.0, 0.0).astype(BF16)

    row_loop(H, ROWS, hot_rows)

    def spread(p):
        for r in range(2):
            w2[p, r * E : (r + 1) * E, :] = mm(dw[2 * p + r], onehot[r]).astype(BF16)

    loads[1].wait()
    for p in range(K // 2):
        spread(p)
    two = []
    for h in range(2):
        for cp in one[h]:
            cp.wait_recv()
        mc_out[h] = mm(mix[h], sec_cols[h]).astype(BF16)
        two.append(exchange(1, h, mc_out, mixed))
    pending += two[0] + two[1]

    def hidden_grad(p):
        g = mm(cotp[:, pl.ds(mult(p * 2 * E, 2 * E), 2 * E)], w2[p]).astype(BF16)
        for k in range(K):
            gh[k, :, pl.ds(mult(p * 128, 128), 128)] = g[:, k * 128 : (k + 1) * 128]

    for p in range(K // 2):
        hidden_grad(p)
    def second_norm(h, n):
        nat, own = aligned(n * ic + h * part), aligned(n * part)
        s = aligned(h * half + n * part)
        resid = (tok[nat, :].astype(F32) + mixed[h, own, :].astype(F32) * opened[nat, :]).astype(BF16).astype(F32)
        inv = lax.rsqrt(jnp.mean(resid * resid, axis=-1, keepdims=True) + epsilon)
        n2 = resid * inv
        norm2[s, :] = n2
        inv2s[s, :] = jnp.broadcast_to(inv, (part, 128))
        inner[s, :] = (n2 * gain2[...]).astype(BF16)

    def mlp(h, k):
        cols = slice(k * E, k * E + E)
        mine = slice(h * half, (h + 1) * half)
        x = inner[mine, cols]
        for c0 in range(0, H, 256):
            cs = slice(c0, c0 + 256)
            va = mm(x, gw[k, :, cs])
            vu = mm(x, uw[k, :, cs])
            for n in range(0, half, 16):
                a, u = va[n : n + 16], vu[n : n + 16]
                t = slice(h * half + n, h * half + n + 16)
                g = gh[k, t, cs].astype(F32)
                sig = 0.5 * jnp.tanh(0.5 * a) + 0.5
                silu = a * sig
                hid[k, t, cs] = (silu * u).astype(BF16)
                gg[k, t, cs] = (g * u * (sig + silu * (1.0 - sig))).astype(BF16)
                gu[k, t, cs] = (g * silu).astype(BF16)
        ginner[mine, cols] = mm(gg[k, mine, :], gw[k], 1, 1) + mm(gu[k, mine, :], uw[k], 1, 1)

    def second_back(h, n):
        nat, own = aligned(n * ic + h * part), aligned(n * part)
        s = aligned(h * half + n * part)
        n2 = norm2[s, :]
        dn = ginner[s, :] * gain2[...]
        mean = jnp.mean(dn * n2, axis=-1, keepdims=True)
        gr = (cot[nat, :].astype(F32) + inv2s[s, 0:1] * (dn - n2 * mean)).astype(BF16)
        gres[nat, :] = gr
        wide = gr.astype(F32)
        op = opened[nat, :]
        gm_out[h, own, :] = (wide * op).astype(BF16)
        gos[nat, :] = wide * mixed[h, own, :].astype(F32) * op * (1.0 - op) * scale1[...]

    three = []
    share = rows // DP
    pr = lax.broadcasted_iota(jnp.int32, (DP * 16, half), 0)
    pc = lax.div(lax.broadcasted_iota(jnp.int32, (DP * 16, half), 1), part)
    pick = (lax.div(pr, 16) == lax.div(pc, nbd)) & (lax.rem(pr, 16) == lax.rem(pc, nbd))
    pick = jnp.where(pick, 1.0, 0.0).astype(BF16)
    four = [None, None]

    def back_mix(h):
        for cp in three[h]:
            cp.wait_recv()
        gs_out[h] = mm(mix_t[h], gm_cols[h]).astype(BF16)
        four[h] = exchange(3, h, gs_out, gs)
        pending.extend(four[h])

    def outer(h):
        both = jnp.where(same, mm(sec_cols[h], gm_cols[h], 1, 1), 0.0).astype(BF16)
        picked = mm(pick, both).astype(BF16)
        for d in range(DP):
            ft[h, d, share : share + 16, :] = picked[d * 16 : (d + 1) * 16, :]

    arrivals = {}
    y_units = ((0, 1),)
    z_units = ((0, 0), (0, 1))

    def start(key, src, dst, send_sem, recv_sem, device):
        cp = pltpu.make_async_remote_copy(
            src_ref=src, dst_ref=dst, send_sem=send_sem, recv_sem=recv_sem, device_id=device, device_id_type=MESH
        )
        cp.start()
        arrivals[key] = cp
        pending.append(cp)

    far_mine = lax.rem(dp + 2, DP)
    far_peer = lax.rem(peer_core + 2, DP)

    def spot(q):
        return (q % 2) * 4 + (q // 2) % 2 * 2 + q // 4

    def down_term(p):
        for r in range(2):
            c = cotp[:, (2 * p + r) * E : (2 * p + r + 1) * E]
            parts = []
            for k in range(K):
                raw = mm(hid[k, :, p * 128 : (p + 1) * 128], c, 0, 0)
                parts.append(raw[r * chunk : (r + 1) * chunk, :])
            size = chunk // S
            for q in range(S):
                piece = jnp.concatenate([v[q * size : (q + 1) * size, :] for v in parts], axis=0)
                ws[0, r, p, spot(q)] = piece.astype(BF16)

    def in_term(j, grads, p):
        for r in range(2):
            x = inner[:, (2 * p + r) * E : (2 * p + r + 1) * E]
            raw = mm(grads[2 * p + r], x, 0, 0).astype(BF16)
            for q in range(S):
                ws[j, r, p, spot(q)] = raw[q * hs : (q + 1) * hs, :]

    def to_core(j):
        for slot, owner in enumerate((far_peer, peer_core)):
            for r in range(2):
                start(
                    ("c", j, r, slot), ws.at[j, r, owner], rc.at[j, r, slot],
                    csend.at[j, r, slot], crecv.at[j, r, slot], {"dp": peer_core},
                )

    def down_terms():
        for p in range(K // 2):
            down_term(p)
        to_core(0)

    def near_sum(j, r, q, slot):
        owner = dp if slot else far_mine
        return ws[j, r, owner, q].astype(F32) + rc[j, r, slot, q].astype(F32)

    def y_first(r):
        for slot in range(2):
            arrivals["c", 0, r, slot].wait_recv()
            for z in range(4):
                yo2[r, slot, z] = near_sum(0, r, (1 - yy) * 4 + z, slot).astype(BF16)
        start(("y", 0, r), yo2.at[r], ry2.at[r], ysend.at[0, r], yrecv.at[0, r], {"seq": me + 1 - 2 * yy})

    def x_second(r):
        arrivals["y", 0, r].wait_recv()
        for z in range(4):
            xo2[r, z] = (near_sum(0, r, yy * 4 + z, 0) + ry2[r, 0, z].astype(F32)).astype(BF16)
        start(("x", 0, r), xo2.at[r], rx2.at[r], xsend.at[0, r], xrecv.at[0, r], {"dp": peer_x})

    def over_x(j, r):
        arrivals["c", j, r, 0].wait_recv()
        for q in range(S):
            xo[j, r, q] = (ws[j, r, far_mine, q].astype(F32) + rc[j, r, 0, q].astype(F32)).astype(BF16)
        start(("x", j, r), xo.at[j, r], rx.at[j, r], xsend.at[j, r], xrecv.at[j, r], {"dp": peer_x})

    def partial(j, r, q):
        return ws[j, r, dp, q].astype(F32) + rc[j, r, 1, q].astype(F32) + rx[j, r, q].astype(F32)

    def over_y(j, r):
        arrivals["c", j, r, 1].wait_recv()
        arrivals["x", j, r].wait_recv()
        for z in range(4):
            yo[j, r, z] = partial(j, r, (1 - yy) * 4 + z).astype(BF16)
        start(("y", j, r), yo.at[j, r], ry.at[j, r], ysend.at[j, r], yrecv.at[j, r], {"seq": me + 1 - 2 * yy})

    def after_y(j, r, z):
        if (j, r) in y_units:
            return near_sum(0, r, yy * 4 + z, 1) + ry2[r, 1, z].astype(F32) + rx2[r, z].astype(F32)
        return partial(j, r, yy * 4 + z) + ry[j, r, z].astype(F32)

    def over_lo(j, r):
        arrivals["x" if (j, r) in y_units else "y", j, r].wait_recv()
        for z in range(2):
            lo[j, r, z] = after_y(j, r, (1 - lo_z) * 2 + z).astype(BF16)
        start(("l", j, r), lo.at[j, r], rl.at[j, r], losend.at[j, r], lorecv.at[j, r], {"seq": me + 2 - 4 * lo_z})

    def after_lo(j, r, z):
        return after_y(j, r, lo_z * 2 + z) + rl[j, r, z].astype(F32)

    def over_hi(j, r):
        arrivals["l", j, r].wait_recv()
        ho[j, r] = after_lo(j, r, 1 - hi_z).astype(BF16)
        start(("h", j, r), ho.at[j, r], rh.at[j, r], hisend.at[j, r], hirecv.at[j, r], {"seq": me + 4 - 8 * hi_z})

    def over_z(j, r):
        arrivals["x" if (j, r) in y_units else "y", j, r].wait_recv()
        for n in range(1, 4):
            z = lax.rem(hi_z * 2 + lo_z + n, 4)
            zo[r, n] = after_y(j, r, lax.rem(z, 2) * 2 + lax.div(z, 2)).astype(BF16)
            start(("z", r, n), zo.at[r, n], rz.at[r, n], zsend.at[r, n], zrecv.at[r, n], {"seq": z * 2 + yy})

    def finish(j, r):
        scale = (DP * rows * S) ** (-0.5)
        if (j, r) in z_units:
            total = after_y(j, r, lo_z * 2 + hi_z)
            for n in range(1, 4):
                arrivals["z", r, n].wait_recv()
                total = total + rz[r, n].astype(F32)
            wout[j, r * hs : (r + 1) * hs, :] = total * scale
            return
        arrivals["h", j, r].wait_recv()
        wout[j, r * hs : (r + 1) * hs, :] = (after_lo(j, r, hi_z) + rh[j, r].astype(F32)) * scale

    def factor(h):
        for cp in four[h]:
            cp.wait_recv()
        f1 = mm(normed[...], gs[h], 1, 1).astype(BF16)
        for d in range(DP):
            ft[h, d, 0:share, :] = f1[d * share : (d + 1) * share, :]
        for r in range(1, DP):
            d = lax.rem(dp + r, DP)
            start(("f", h, r), ft.at[h, d], rf.at[h, r], fsend.at[h, r], frecv.at[h, r], {"dp": d})

    def first_back(s):
        v = tok[s, :].astype(F32)
        inv = lax.rsqrt(jnp.mean(v * v, axis=-1, keepdims=True) + epsilon)
        n1 = v * inv
        dm = (ginner[s, :] + gos[s, :]) * gain1[...]
        mean = jnp.mean(dm * n1, axis=-1, keepdims=True)
        gtok[s, :] = (gres[s, :].astype(F32) + inv * (dm - n1 * mean)).astype(BF16)

    def token_grad():
        ginner[...] = mm(ffp[...], gs[...].reshape(rows, width), 0, 0)
        row_loop(rows, ROWS, first_back)

    def factor_sum(h):
        for r in range(1, DP):
            arrivals["f", h, r].wait_recv()
        total = ft[h, dp].astype(F32)
        for r in range(1, DP):
            total = total + rf[h, r].astype(F32)
        facs[:, h * half : (h + 1) * half] = total * ((DP * width) ** (-0.5))

    loads[2].wait()
    loads[3].wait()
    for h in range(2):
        for cp in two[h]:
            cp.wait_recv()
        for n in range(S):
            second_norm(h, n)
        for k in range(K):
            mlp(h, k)
            if h == 1 and k % 2 == 1:
                in_term(1, gg, k // 2)
                in_term(2, gu, k // 2)
        if h == 1:
            to_core(1)
            to_core(2)
        for n in range(S):
            second_back(h, n)
        three.append(exchange(2, h, gm_out, gm_cols))
    pending += three[0] + three[1]
    over_x(1, 0)
    over_x(1, 1)
    over_x(2, 0)
    over_x(2, 1)
    down_terms()
    back_mix(0)
    over_x(0, 0)
    y_first(1)
    outer(0)
    back_mix(1)
    outer(1)
    over_y(1, 0)
    over_y(1, 1)
    over_y(2, 0)
    x_second(1)
    over_y(2, 1)
    factor(0)
    factor(1)
    over_lo(1, 0)
    over_lo(1, 1)
    over_y(0, 0)
    over_lo(2, 0)
    over_lo(2, 1)
    over_z(0, 1)
    token_grad()
    over_hi(1, 0)
    over_hi(1, 1)
    over_hi(2, 0)
    over_hi(2, 1)
    over_z(0, 0)
    factor_sum(0)
    factor_sum(1)
    finish(1, 0)
    finish(1, 1)
    finish(2, 0)
    finish(2, 1)
    finish(0, 0)
    finish(0, 1)
    for cp in pending:
        cp.wait_send()


def arrange(S, share, part, kd, step, gtok_in, facs, wout, gtok, first, second, gate, up, down):
    gtok[...] = gtok_in[...]
    nbd = second.shape[1]
    half = S * part
    pieces = [facs[0:share, h * half + q * part : h * half + (q + 1) * part] for q in range(S) for h in range(2)]
    first[...] = jnp.concatenate(pieces, axis=1)
    for c in range(S):
        pieces = [facs[share : share + nbd, h * half + c * part : h * half + (c + 1) * part] for h in range(2)]
        second[c] = jnp.concatenate(pieces, axis=1)
    gate[...] = wout[1]
    up[...] = wout[2]
    size = wout.shape[1] // kd
    K = size // step
    for d in range(kd):
        for k in range(K):
            at = d * size + k * step
            down[pl.ds(d * size + k, step, stride=K), :] = wout[0, at : at + step, :]


def fused_body(
    tokens, cotangent, first_factor, second_factor, norm_gain, gate_scale, gate_bias, mlp_gain,
    gate_weight, up_weight, down_weight,
):
    S, DP = lax.axis_size("seq"), lax.axis_size("dp")
    rows, width = tokens.shape[1:]
    K, E, H = gate_weight.shape
    ic = rows // S
    nbd = S // DP
    hs = H // S
    kd = K // DP
    share = rows // DP
    part = ic // 2
    split = jnp.transpose(second_factor, (0, 2, 1))
    gains = [v.reshape(1, width) for v in (norm_gain, gate_scale, gate_bias, mlp_gain)]
    full = (rows, width)
    vm = pltpu.VMEM
    fourth = vm((2, 4, hs, E), BF16)
    owned = vm((3, 2, S, hs, E), BF16)
    wide = vm(full, F32)
    half = vm(full, BF16)
    pair = vm((2, rows // 2, width), BF16)
    deep = vm((K, rows, H), BF16)
    dma = pltpu.SemaphoreType.DMA
    scratch = [
        half, pair, pair, pair, pair, wide, pair, pair, pair, pair,
        vm((2, rows // 2, rows // 2), BF16), vm((2, rows // 2, rows // 2), BF16), vm((2, H, K * 128), BF16),
        vm((K // 2, 2 * E, K * 128), BF16), deep, deep, deep, deep,
        half, wide, vm((rows, 128), F32), wide, wide, half,
        half, vm((K, E, H), BF16), vm((K, E, H), BF16), vm((K, E, H), BF16),
        half, vm((rows, rows), BF16), vm((3, 2, DP, S, hs, E), BF16), vm((3, 2, 2, S, hs, E), BF16), owned, owned,
        vm((3, 2, 4, hs, E), BF16), vm((3, 2, 4, hs, E), BF16), fourth, fourth, vm((2, 2, 4, hs, E), BF16), vm((2, 2, 4, hs, E), BF16), fourth, fourth, vm((3, 2, 2, hs, E), BF16), vm((3, 2, 2, hs, E), BF16),
        vm((3, 2, hs, E), BF16), vm((3, 2, hs, E), BF16),
        vm((2, DP, share + 16, rows // 2), BF16), vm((2, DP, share + 16, rows // 2), BF16),
        dma((4, 2, S)), dma((4, 2, S)), dma((3, 2, 2)), dma((3, 2, 2)), dma((3, 2)), dma((3, 2)),
        dma((3, 2)), dma((3, 2)), dma((3, 2)), dma((3, 2)), dma((3, 2)), dma((3, 2)), dma((2, DP)), dma((2, DP)), dma((2, 4)), dma((2, 4)), dma((4,)),
    ]
    whole = pl.BlockSpec(memory_space=pltpu.VMEM)
    away = pl.BlockSpec(memory_space=pl.ANY)
    gtok, facs, wout = pl.pallas_call(
        lambda *refs: fused(S, DP, *refs),
        out_shape=(
            jax.ShapeDtypeStruct(full, BF16),
            jax.ShapeDtypeStruct((share + 16, rows), F32),
            jax.ShapeDtypeStruct((3, kd * hs, E), F32),
        ),
        in_specs=[whole, away] + [whole] * 6 + [away] * 3,
        out_specs=(whole,) * 3,
        scratch_shapes=scratch,
        compiler_params=pltpu.CompilerParams(
            collective_id=0, has_side_effects=True, vmem_limit_bytes=62 * 1024 * 1024
        ),
    )(tokens[0], cotangent[0], first_factor[0], split, *gains, gate_weight, up_weight, down_weight)
    outs = pl.pallas_call(
        lambda *refs: arrange(S, share, part, kd, hs // K, *refs),
        out_shape=(
            jax.ShapeDtypeStruct(full, BF16),
            jax.ShapeDtypeStruct((share, rows), F32),
            jax.ShapeDtypeStruct((S, nbd, ic), F32),
            jax.ShapeDtypeStruct((kd * hs, E), F32),
            jax.ShapeDtypeStruct((kd * hs, E), F32),
            jax.ShapeDtypeStruct((kd * hs, E), F32),
        ),
        in_specs=[whole] * 3,
        out_specs=(whole,) * 6,
    )(gtok, facs, wout)
    gtok, first, second, gate, up, down = outs
    gate, up, down = [jnp.transpose(w.reshape(kd, hs, E), (0, 2, 1)) for w in (gate, up, down)]
    return gtok[None], first.T[None], jnp.transpose(second, (0, 2, 1)), gate, up, down


def body(*args):
    S, DP = lax.axis_size("seq"), lax.axis_size("dp")
    blocks, rows = args[2].shape[:2]
    K, E, H = args[8].shape
    fits = (
        S == 8 and blocks == 1 and args[0].shape[0] == 1 and args[0].shape[1] == rows and rows == S * 2 * ROWS
        and DP == 4 and S % DP == 0 and S // DP <= 16 and S <= 128
        and E == 128 and H == K * 64 and K == 2 * DP and 64 % (8 * S) == 0
    )
    return fused_body(*args) if fits else plain_body(*args)


def solution(mesh):
    placed = (
        P("dp", "seq", None),
        P("dp", "seq", None),
        P("seq", None, None),
        P(None, "seq", None),
        P(),
        P(),
        P(),
        P(),
        P(),
        P(),
        P(),
    )
    return jax.shard_map(
        body,
        mesh=mesh,
        in_specs=placed,
        out_specs=(
            P("dp", "seq", None),
            P("seq", None, "dp"),
            P(None, "seq", "dp"),
            P("dp", None, "seq"),
            P("dp", None, "seq"),
            P("dp", None, "seq"),
        ),
        check_vma=False,
    )
```

```python
import jax
import jax.numpy as jnp
from jax import lax
from jax.experimental import pallas as pl
from jax.experimental.pallas import tpu as pltpu
from jax.sharding import PartitionSpec as P

epsilon = 1e-05


def inverse_rms(values):
    return lax.rsqrt(jnp.mean(values * values, axis=-1, keepdims=True) + epsilon)


def norm_backward(grad_normed, normed_values, inverse):
    return inverse * (
        grad_normed - normed_values * jnp.mean(grad_normed * normed_values, axis=-1, keepdims=True)
    )


def plain_body(
    tokens,
    cotangent,
    first_factor,
    second_factor,
    norm_gain,
    gate_scale,
    gate_bias,
    mlp_gain,
    gate_weight,
    up_weight,
    down_weight,
):
    inputs = tokens[0]
    upstream = cotangent[0]
    rows_local, width = inputs.shape
    local_blocks, block_size = (first_factor.shape[0], first_factor.shape[1])
    mlp_blocks, block_in, block_hidden = gate_weight.shape
    inputs_wide = inputs.astype(jnp.float32)
    first_inverse = inverse_rms(inputs_wide)
    first_normed = inputs_wide * first_inverse
    normed_tokens = (first_normed * norm_gain).astype(jnp.bfloat16)
    blocked = normed_tokens.reshape(local_blocks, block_size, width)
    section_one = jnp.einsum(
        "bij,bjd->bid", first_factor, blocked, preferred_element_type=jnp.float32
    ).astype(jnp.bfloat16)
    section_cols = lax.all_to_all(section_one, "seq", split_axis=1, concat_axis=0, tiled=True)
    mixed_cols = jnp.einsum(
        "cib,bid->cid", second_factor, section_cols, preferred_element_type=jnp.float32
    ).astype(jnp.bfloat16)
    mixed_rows = lax.all_to_all(mixed_cols, "seq", split_axis=0, concat_axis=1, tiled=True).reshape(
        rows_local, width
    )
    mixed_wide = mixed_rows.astype(jnp.float32)
    gate_open = jax.nn.sigmoid(normed_tokens.astype(jnp.float32) * gate_scale + gate_bias)
    after_mix = (inputs_wide + mixed_wide * gate_open).astype(jnp.bfloat16)
    after_wide = after_mix.astype(jnp.float32)
    second_inverse = inverse_rms(after_wide)
    second_normed = after_wide * second_inverse
    mlp_input = (
        (second_normed * mlp_gain).astype(jnp.bfloat16).reshape(rows_local, mlp_blocks, block_in)
    )
    pre_gate = jnp.einsum(
        "tkd,kdh->tkh", mlp_input, gate_weight, preferred_element_type=jnp.float32
    )
    pre_up = jnp.einsum("tkd,kdh->tkh", mlp_input, up_weight, preferred_element_type=jnp.float32)
    sig_gate = jax.nn.sigmoid(pre_gate)
    hidden = (pre_gate * sig_gate * pre_up).astype(jnp.bfloat16)
    permuted = jnp.transpose(hidden, (0, 2, 1)).reshape(rows_local, mlp_blocks, block_hidden)
    upstream_wide = upstream.astype(jnp.float32)
    upstream_blocks = upstream.reshape(rows_local, mlp_blocks, block_in)
    grad_perm = jnp.einsum(
        "tkd,kdh->tkh", upstream_blocks, down_weight, preferred_element_type=jnp.float32
    ).astype(jnp.bfloat16)
    grad_hidden = jnp.transpose(
        grad_perm.reshape(rows_local, block_hidden, mlp_blocks), (0, 2, 1)
    ).astype(jnp.float32)
    grad_gate_pre = (grad_hidden * pre_up * sig_gate * (1.0 + pre_gate * (1.0 - sig_gate))).astype(
        jnp.bfloat16
    )
    grad_up_pre = (grad_hidden * pre_gate * sig_gate).astype(jnp.bfloat16)
    grad_inner = jnp.einsum(
        "tkh,kdh->tkd", grad_gate_pre, gate_weight, preferred_element_type=jnp.float32
    )
    grad_inner = grad_inner + jnp.einsum(
        "tkh,kdh->tkd", grad_up_pre, up_weight, preferred_element_type=jnp.float32
    )
    grad_inner = grad_inner.reshape(rows_local, width)
    grad_after = (
        upstream_wide + norm_backward(grad_inner * mlp_gain, second_normed, second_inverse)
    ).astype(jnp.bfloat16)
    grad_after_wide = grad_after.astype(jnp.float32)
    grad_mixed = (grad_after_wide * gate_open).astype(jnp.bfloat16)
    grad_open = grad_after_wide * mixed_wide * gate_open * (1.0 - gate_open)
    grad_mixed_cols = lax.all_to_all(
        grad_mixed.reshape(local_blocks, block_size, width),
        "seq",
        split_axis=1,
        concat_axis=0,
        tiled=True,
    )
    grad_section_cols = jnp.einsum(
        "cib,cid->bid", second_factor, grad_mixed_cols, preferred_element_type=jnp.float32
    ).astype(jnp.bfloat16)
    second_term = jnp.einsum(
        "cid,bid->cib", grad_mixed_cols, section_cols, preferred_element_type=jnp.float32
    )
    grad_section = lax.all_to_all(grad_section_cols, "seq", split_axis=0, concat_axis=1, tiled=True)
    first_term = jnp.einsum(
        "bid,bjd->bij", grad_section, blocked, preferred_element_type=jnp.float32
    )
    grad_normed = jnp.einsum(
        "bij,bid->bjd", first_factor, grad_section, preferred_element_type=jnp.float32
    ).reshape(rows_local, width)
    grad_normed = grad_normed + grad_open * gate_scale
    grad_inputs = (
        grad_after_wide + norm_backward(grad_normed * norm_gain, first_normed, first_inverse)
    ).astype(jnp.bfloat16)
    factor_first, factor_second = (
        lax.psum_scatter(
            first_term.astype(jnp.bfloat16), "dp", scatter_dimension=2, tiled=True
        ).astype(jnp.float32),
        lax.psum_scatter(
            second_term.astype(jnp.bfloat16), "dp", scatter_dimension=2, tiled=True
        ).astype(jnp.float32),
    )
    replicas = lax.axis_size("dp")
    factor_weight = (replicas * width) ** (-0.5)
    mlp_weight = (replicas * rows_local * lax.axis_size("seq")) ** (-0.5)
    gate_term = jnp.einsum(
        "tkd,tkh->kdh", mlp_input, grad_gate_pre, preferred_element_type=jnp.float32
    )
    up_term = jnp.einsum("tkd,tkh->kdh", mlp_input, grad_up_pre, preferred_element_type=jnp.float32)
    down_term = jnp.einsum(
        "tkd,tkh->kdh", upstream_blocks, permuted, preferred_element_type=jnp.float32
    )
    stacked = jnp.concatenate([gate_term, up_term, down_term], axis=1)
    seq_summed = lax.psum_scatter(stacked, "seq", scatter_dimension=2, tiled=True)
    reduced = lax.psum_scatter(seq_summed, "dp", scatter_dimension=0, tiled=True)
    reduced = reduced * mlp_weight
    grad_gate = reduced[:, 0:block_in, :]
    grad_up = reduced[:, block_in : 2 * block_in, :]
    grad_down = reduced[:, 2 * block_in : 3 * block_in, :]
    return (
        grad_inputs[None],
        factor_first * factor_weight,
        factor_second * factor_weight,
        grad_gate,
        grad_up,
        grad_down,
    )


MESH = pl.DeviceIdType.MESH
F32 = jnp.float32
BF16 = jnp.bfloat16
ROWS = 16
UNR = 8


def mm(a, b, da=1, db=0):
    return lax.dot_general(a, b, (((da,), (db,)), ((), ())), preferred_element_type=F32)


def mult(v, m):
    return v if isinstance(v, int) else pl.multiple_of(v, m)


def row_loop(total, step, fn):
    def one(n, carry):
        fn(pl.ds(mult(n * step, step), step))
        return carry

    lax.fori_loop(0, total // step, one, 0, unroll=UNR)


def count_loop(total, fn):
    def one(n, carry):
        fn(n)
        return carry

    lax.fori_loop(0, total, one, 0)


def fused(
    S, DP,
    tok, cot_in, ff, sf, gain1, scale1, bias1, gain2, gw_in, uw_in, dw_in,
    gtok, facs, wout,
    normed, sec_out, sec_cols, mc_out, mixed, opened, gm_out, gm_cols, gs_out, gs,
    mix, mix_t, onehot, w2, gh, hid, gg, gu, inner, norm2, inv2s, ginner, gos, gres,
    cot, gw, uw, dw, cotp, ffp, ws, rc, xo, rx, yo, ry, xo2, rx2, yo2, ry2, zo, rz, lo, rl, ho, rh, ft, rf,
    send, recv, csend, crecv, xsend, xrecv, ysend, yrecv, losend, lorecv, hisend, hirecv, fsend, frecv, zsend, zrecv, lsem,
):
    me = lax.axis_index("seq")
    dp = lax.axis_index("dp")
    core = lax.rem(dp, 2)
    peer_core = dp + 1 - 2 * core
    peer_x = lax.rem(dp + 2, DP)
    rows, width = tok.shape
    K, E, H = gw.shape
    chunk = H // K
    ic = rows // S
    hs = H // S
    nbd = S // DP
    kd = K // DP
    half = rows // 2
    part = ic // 2
    ZS = S // 2
    yy = lax.rem(me, 2)
    lo_z = lax.rem(lax.div(me, 2), 2)
    hi_z = lax.div(me, 4)

    loads = []
    for n, (a, b) in enumerate(((cot_in, cot), (dw_in, dw), (gw_in, gw), (uw_in, uw))):
        load = pltpu.make_async_copy(a, b, lsem.at[n])
        load.start()
        loads.append(load)
    barrier = pltpu.get_barrier_semaphore()
    for r in range(1, S):
        pl.semaphore_signal(barrier, inc=1, device_id={"seq": lax.rem(me + r, S)}, device_id_type=MESH)
    for r in range(1, DP):
        pl.semaphore_signal(barrier, inc=1, device_id={"dp": lax.rem(dp + r, DP)}, device_id_type=MESH)

    def first_norm(s):
        v = tok[s, :].astype(F32)
        inv = lax.rsqrt(jnp.mean(v * v, axis=-1, keepdims=True) + epsilon)
        normed[s, :] = (v * inv * gain1[...]).astype(BF16)

    row_loop(rows, ROWS, first_norm)
    for q in range(S):
        for h in range(2):
            ffp[h * half + q * part : h * half + (q + 1) * part, :] = ff[q * ic + h * part : q * ic + (h + 1) * part, :]

    def aligned(start):
        return pl.ds(mult(start, part), part)

    def exchange(phase, h, src, dst):
        def where(ref, q):
            return ref.at[h, aligned(q * part)]

        copies = []
        for r in sorted(range(1, S), key=lambda r: abs(r - S // 2)):
            q = lax.rem(me + r, S)
            cp = pltpu.make_async_remote_copy(
                src_ref=where(src, q),
                dst_ref=where(dst, me),
                send_sem=send.at[phase, h, r],
                recv_sem=recv.at[phase, h, r],
                device_id={"seq": q},
                device_id_type=MESH,
            )
            cp.start()
            copies.append(cp)
        where(dst, me)[...] = where(src, me)[...]
        return copies

    pending = []
    one = []
    for h in range(2):
        sec_out[h] = mm(ffp[h * half : (h + 1) * half, :], normed[...]).astype(BF16)
        if h == 0:
            pl.semaphore_wait(barrier, S - 1 + DP - 1)
        one.append(exchange(0, h, sec_out, sec_cols))
    pending += one[0] + one[1]

    def open_gate(s):
        opened[s, :] = jax.nn.sigmoid(normed[s, :].astype(F32) * scale1[...] + bias1[...])

    row_loop(rows, ROWS, open_gate)
    ri = lax.broadcasted_iota(jnp.int32, (half, half), 0)
    ci = lax.broadcasted_iota(jnp.int32, (half, half), 1)
    same = lax.rem(ri, part) == lax.rem(ci, part)
    er = lax.broadcasted_iota(jnp.int32, (half, S), 0)
    ec = lax.broadcasted_iota(jnp.int32, (half, S), 1)
    expand = jnp.where(lax.div(er, part) == ec, 1.0, 0.0).astype(BF16)
    pi = lax.broadcasted_iota(jnp.int32, (part, half), 0)
    pj = lax.rem(lax.broadcasted_iota(jnp.int32, (part, half), 1), part)
    for c in range(S):
        spread_c = mm(sf[c], expand, 0, 1)
        for h in range(2):
            rows_c = jnp.where(pi == pj, spread_c[h * part : (h + 1) * part, :], 0.0)
            mix[h, c * part : (c + 1) * part, :] = rows_c.astype(BF16)
    for h in range(2):
        mix_t[h] = jnp.transpose(mix[h].astype(F32)).astype(BF16)

    def regroup(n):
        for h in range(2):
            cotp[aligned(h * half + n * part), :] = cot[aligned(n * ic + h * part), :]

    loads[0].wait()
    count_loop(S, regroup)

    def hot_rows(s):
        hi = lax.broadcasted_iota(jnp.int32, (ROWS, K * 128), 0) + s.start
        hc = lax.broadcasted_iota(jnp.int32, (ROWS, K * 128), 1)
        lane = lax.rem(hc, 128)
        hit = hi == lax.rem(lane, chunk) * K + lax.div(hc, 128)
        for r in range(2):
            onehot[r, s, :] = jnp.where(hit & (lax.div(lane, chunk) == r), 1.0, 0.0).astype(BF16)

    row_loop(H, ROWS, hot_rows)

    def spread(p):
        for r in range(2):
            w2[p, r * E : (r + 1) * E, :] = mm(dw[2 * p + r], onehot[r]).astype(BF16)

    loads[1].wait()
    for p in range(K // 2):
        spread(p)
    two = []
    for h in range(2):
        for cp in one[h]:
            cp.wait_recv()
        mc_out[h] = mm(mix[h], sec_cols[h]).astype(BF16)
        two.append(exchange(1, h, mc_out, mixed))
    pending += two[0] + two[1]

    def hidden_grad(p):
        g = mm(cotp[:, pl.ds(mult(p * 2 * E, 2 * E), 2 * E)], w2[p]).astype(BF16)
        for k in range(K):
            gh[k, :, pl.ds(mult(p * 128, 128), 128)] = g[:, k * 128 : (k + 1) * 128]

    for p in range(K // 2):
        hidden_grad(p)
    def second_norm(h, n):
        nat, own = aligned(n * ic + h * part), aligned(n * part)
        s = aligned(h * half + n * part)
        resid = (tok[nat, :].astype(F32) + mixed[h, own, :].astype(F32) * opened[nat, :]).astype(BF16).astype(F32)
        inv = lax.rsqrt(jnp.mean(resid * resid, axis=-1, keepdims=True) + epsilon)
        n2 = resid * inv
        norm2[s, :] = n2
        inv2s[s, :] = jnp.broadcast_to(inv, (part, 128))
        inner[s, :] = (n2 * gain2[...]).astype(BF16)

    def mlp(h, k):
        cols = slice(k * E, k * E + E)
        mine = slice(h * half, (h + 1) * half)
        x = inner[mine, cols]
        for c0 in range(0, H, 256):
            cs = slice(c0, c0 + 256)
            va = mm(x, gw[k, :, cs])
            vu = mm(x, uw[k, :, cs])
            for n in range(0, half, 16):
                a, u = va[n : n + 16], vu[n : n + 16]
                t = slice(h * half + n, h * half + n + 16)
                g = gh[k, t, cs].astype(F32)
                sig = 0.5 * jnp.tanh(0.5 * a) + 0.5
                silu = a * sig
                hid[k, t, cs] = (silu * u).astype(BF16)
                gg[k, t, cs] = (g * u * (sig + silu * (1.0 - sig))).astype(BF16)
                gu[k, t, cs] = (g * silu).astype(BF16)
        ginner[mine, cols] = mm(gg[k, mine, :], gw[k], 1, 1) + mm(gu[k, mine, :], uw[k], 1, 1)

    def second_back(h, n):
        nat, own = aligned(n * ic + h * part), aligned(n * part)
        s = aligned(h * half + n * part)
        n2 = norm2[s, :]
        dn = ginner[s, :] * gain2[...]
        mean = jnp.mean(dn * n2, axis=-1, keepdims=True)
        gr = (cot[nat, :].astype(F32) + inv2s[s, 0:1] * (dn - n2 * mean)).astype(BF16)
        gres[nat, :] = gr
        wide = gr.astype(F32)
        op = opened[nat, :]
        gm_out[h, own, :] = (wide * op).astype(BF16)
        gos[nat, :] = wide * mixed[h, own, :].astype(F32) * op * (1.0 - op) * scale1[...]

    three = []
    share = rows // DP
    pr = lax.broadcasted_iota(jnp.int32, (DP * 16, half), 0)
    pc = lax.div(lax.broadcasted_iota(jnp.int32, (DP * 16, half), 1), part)
    pick = (lax.div(pr, 16) == lax.div(pc, nbd)) & (lax.rem(pr, 16) == lax.rem(pc, nbd))
    pick = jnp.where(pick, 1.0, 0.0).astype(BF16)
    four = [None, None]

    def back_mix(h):
        for cp in three[h]:
            cp.wait_recv()
        gs_out[h] = mm(mix_t[h], gm_cols[h]).astype(BF16)
        four[h] = exchange(3, h, gs_out, gs)
        pending.extend(four[h])

    def outer(h):
        both = jnp.where(same, mm(sec_cols[h], gm_cols[h], 1, 1), 0.0).astype(BF16)
        picked = mm(pick, both).astype(BF16)
        for d in range(DP):
            ft[h, d, share : share + 16, :] = picked[d * 16 : (d + 1) * 16, :]

    arrivals = {}
    y_units = ((0, 1),)
    z_units = ((0, 0), (0, 1), (1, 0), (1, 1), (2, 0), (2, 1))
    early = []

    def mark():
        early.extend(pending)
        pending.clear()

    def drain():
        for cp in early:
            cp.wait_send()

    def start(key, src, dst, send_sem, recv_sem, device):
        cp = pltpu.make_async_remote_copy(
            src_ref=src, dst_ref=dst, send_sem=send_sem, recv_sem=recv_sem, device_id=device, device_id_type=MESH
        )
        cp.start()
        arrivals[key] = cp
        pending.append(cp)

    far_mine = lax.rem(dp + 2, DP)
    far_peer = lax.rem(peer_core + 2, DP)

    def spot(q):
        return (q % 2) * 4 + (q // 2) % 2 * 2 + q // 4

    def down_term(p):
        for r in range(2):
            c = cotp[:, (2 * p + r) * E : (2 * p + r + 1) * E]
            parts = []
            for k in range(K):
                raw = mm(hid[k, :, p * 128 : (p + 1) * 128], c, 0, 0)
                parts.append(raw[r * chunk : (r + 1) * chunk, :])
            size = chunk // S
            for q in range(S):
                piece = jnp.concatenate([v[q * size : (q + 1) * size, :] for v in parts], axis=0)
                ws[0, r, p, spot(q)] = piece.astype(BF16)

    def in_term(j, grads, p):
        for r in range(2):
            x = inner[:, (2 * p + r) * E : (2 * p + r + 1) * E]
            raw = mm(grads[2 * p + r], x, 0, 0).astype(BF16)
            for q in range(S):
                ws[j, r, p, spot(q)] = raw[q * hs : (q + 1) * hs, :]

    def to_core(j):
        for slot, owner in enumerate((far_peer, peer_core)):
            for r in range(2):
                start(
                    ("c", j, r, slot), ws.at[j, r, owner], rc.at[j, r, slot],
                    csend.at[j, r, slot], crecv.at[j, r, slot], {"dp": peer_core},
                )

    def down_terms():
        for p in range(K // 2):
            down_term(p)
        to_core(0)

    def near_sum(j, r, q, slot):
        owner = dp if slot else far_mine
        return ws[j, r, owner, q].astype(F32) + rc[j, r, slot, q].astype(F32)

    def y_first(r):
        for slot in range(2):
            arrivals["c", 0, r, slot].wait_recv()
            for z in range(4):
                yo2[r, slot, z] = near_sum(0, r, (1 - yy) * 4 + z, slot).astype(BF16)
        start(("y", 0, r), yo2.at[r], ry2.at[r], ysend.at[0, r], yrecv.at[0, r], {"seq": me + 1 - 2 * yy})

    def x_second(r):
        arrivals["y", 0, r].wait_recv()
        for z in range(4):
            xo2[r, z] = (near_sum(0, r, yy * 4 + z, 0) + ry2[r, 0, z].astype(F32)).astype(BF16)
        start(("x", 0, r), xo2.at[r], rx2.at[r], xsend.at[0, r], xrecv.at[0, r], {"dp": peer_x})

    def over_x(j, r):
        arrivals["c", j, r, 0].wait_recv()
        for q in range(S):
            xo[j, r, q] = (ws[j, r, far_mine, q].astype(F32) + rc[j, r, 0, q].astype(F32)).astype(BF16)
        start(("x", j, r), xo.at[j, r], rx.at[j, r], xsend.at[j, r], xrecv.at[j, r], {"dp": peer_x})

    def partial(j, r, q):
        return ws[j, r, dp, q].astype(F32) + rc[j, r, 1, q].astype(F32) + rx[j, r, q].astype(F32)

    def over_y(j, r):
        arrivals["c", j, r, 1].wait_recv()
        arrivals["x", j, r].wait_recv()
        for z in range(4):
            yo[j, r, z] = partial(j, r, (1 - yy) * 4 + z).astype(BF16)
        start(("y", j, r), yo.at[j, r], ry.at[j, r], ysend.at[j, r], yrecv.at[j, r], {"seq": me + 1 - 2 * yy})

    def after_y(j, r, z):
        if (j, r) in y_units:
            return near_sum(0, r, yy * 4 + z, 1) + ry2[r, 1, z].astype(F32) + rx2[r, z].astype(F32)
        return partial(j, r, yy * 4 + z) + ry[j, r, z].astype(F32)

    def over_lo(j, r):
        arrivals["x" if (j, r) in y_units else "y", j, r].wait_recv()
        for z in range(2):
            lo[j, r, z] = after_y(j, r, (1 - lo_z) * 2 + z).astype(BF16)
        start(("l", j, r), lo.at[j, r], rl.at[j, r], losend.at[j, r], lorecv.at[j, r], {"seq": me + 2 - 4 * lo_z})

    def after_lo(j, r, z):
        return after_y(j, r, lo_z * 2 + z) + rl[j, r, z].astype(F32)

    def over_hi(j, r):
        arrivals["l", j, r].wait_recv()
        ho[j, r] = after_lo(j, r, 1 - hi_z).astype(BF16)
        start(("h", j, r), ho.at[j, r], rh.at[j, r], hisend.at[j, r], hirecv.at[j, r], {"seq": me + 4 - 8 * hi_z})

    def over_z(j, r):
        arrivals["x" if (j, r) in y_units else "y", j, r].wait_recv()
        for n in range(1, 4):
            z = lax.rem(hi_z * 2 + lo_z + n, 4)
            zo[j, r, n] = after_y(j, r, lax.rem(z, 2) * 2 + lax.div(z, 2)).astype(BF16)
            start(("z", j, r, n), zo.at[j, r, n], rz.at[j, r, n], zsend.at[j, r, n], zrecv.at[j, r, n], {"seq": z * 2 + yy})

    def finish(j, r):
        scale = (DP * rows * S) ** (-0.5)
        if (j, r) in z_units:
            total = after_y(j, r, lo_z * 2 + hi_z)
            for n in range(1, 4):
                arrivals["z", j, r, n].wait_recv()
                total = total + rz[j, r, n].astype(F32)
            wout[j, r * hs : (r + 1) * hs, :] = total * scale
            return
        arrivals["h", j, r].wait_recv()
        wout[j, r * hs : (r + 1) * hs, :] = (after_lo(j, r, hi_z) + rh[j, r].astype(F32)) * scale

    def factor(h):
        for cp in four[h]:
            cp.wait_recv()
        f1 = mm(normed[...], gs[h], 1, 1).astype(BF16)
        for d in range(DP):
            ft[h, d, 0:share, :] = f1[d * share : (d + 1) * share, :]
        for r in range(1, DP):
            d = lax.rem(dp + r, DP)
            start(("f", h, r), ft.at[h, d], rf.at[h, r], fsend.at[h, r], frecv.at[h, r], {"dp": d})

    def first_back(s):
        v = tok[s, :].astype(F32)
        inv = lax.rsqrt(jnp.mean(v * v, axis=-1, keepdims=True) + epsilon)
        n1 = v * inv
        dm = (ginner[s, :] + gos[s, :]) * gain1[...]
        mean = jnp.mean(dm * n1, axis=-1, keepdims=True)
        gtok[s, :] = (gres[s, :].astype(F32) + inv * (dm - n1 * mean)).astype(BF16)

    def token_grad():
        ginner[...] = mm(ffp[...], gs[...].reshape(rows, width), 0, 0)
        row_loop(rows, ROWS, first_back)

    def factor_sum(h):
        for r in range(1, DP):
            arrivals["f", h, r].wait_recv()
        total = ft[h, dp].astype(F32)
        for r in range(1, DP):
            total = total + rf[h, r].astype(F32)
        facs[:, h * half : (h + 1) * half] = total * ((DP * width) ** (-0.5))

    loads[2].wait()
    loads[3].wait()
    for h in range(2):
        for cp in two[h]:
            cp.wait_recv()
        for n in range(S):
            second_norm(h, n)
        for k in range(K):
            mlp(h, k)
            if h == 1 and k % 2 == 1:
                in_term(1, gg, k // 2)
                in_term(2, gu, k // 2)
        if h == 1:
            to_core(1)
            to_core(2)
        for n in range(S):
            second_back(h, n)
        three.append(exchange(2, h, gm_out, gm_cols))
    pending += three[0] + three[1]
    over_x(1, 0)
    over_x(1, 1)
    over_x(2, 0)
    over_x(2, 1)
    down_terms()
    mark()
    back_mix(0)
    over_x(0, 0)
    y_first(1)
    outer(0)
    back_mix(1)
    outer(1)
    over_y(1, 0)
    over_y(1, 1)
    over_y(2, 0)
    x_second(1)
    over_y(2, 1)
    over_z(1, 0)
    over_z(1, 1)
    factor(0)
    over_z(2, 0)
    drain()
    factor(1)
    over_z(2, 1)
    over_y(0, 0)
    over_z(0, 1)
    token_grad()
    over_z(0, 0)
    finish(1, 0)
    finish(1, 1)
    finish(2, 0)
    factor_sum(0)
    finish(2, 1)
    factor_sum(1)
    finish(0, 1)
    finish(0, 0)
    for cp in pending:
        cp.wait_send()


def arrange(S, share, part, kd, step, gtok_in, facs, wout, gtok, first, second, gate, up, down):
    gtok[...] = gtok_in[...]
    nbd = second.shape[1]
    half = S * part
    pieces = [facs[0:share, h * half + q * part : h * half + (q + 1) * part] for q in range(S) for h in range(2)]
    first[...] = jnp.concatenate(pieces, axis=1)
    for c in range(S):
        pieces = [facs[share : share + nbd, h * half + c * part : h * half + (c + 1) * part] for h in range(2)]
        second[c] = jnp.concatenate(pieces, axis=1)
    gate[...] = wout[1]
    up[...] = wout[2]
    size = wout.shape[1] // kd
    K = size // step
    for d in range(kd):
        for k in range(K):
            at = d * size + k * step
            down[pl.ds(d * size + k, step, stride=K), :] = wout[0, at : at + step, :]


def fused_body(
    tokens, cotangent, first_factor, second_factor, norm_gain, gate_scale, gate_bias, mlp_gain,
    gate_weight, up_weight, down_weight,
):
    S, DP = lax.axis_size("seq"), lax.axis_size("dp")
    rows, width = tokens.shape[1:]
    K, E, H = gate_weight.shape
    ic = rows // S
    nbd = S // DP
    hs = H // S
    kd = K // DP
    share = rows // DP
    part = ic // 2
    split = jnp.transpose(second_factor, (0, 2, 1))
    gains = [v.reshape(1, width) for v in (norm_gain, gate_scale, gate_bias, mlp_gain)]
    full = (rows, width)
    vm = pltpu.VMEM
    fourth = vm((2, 4, hs, E), BF16)
    owned = vm((3, 2, S, hs, E), BF16)
    wide = vm(full, F32)
    half = vm(full, BF16)
    pair = vm((2, rows // 2, width), BF16)
    deep = vm((K, rows, H), BF16)
    dma = pltpu.SemaphoreType.DMA
    scratch = [
        half, pair, pair, pair, pair, wide, pair, pair, pair, pair,
        vm((2, rows // 2, rows // 2), BF16), vm((2, rows // 2, rows // 2), BF16), vm((2, H, K * 128), BF16),
        vm((K // 2, 2 * E, K * 128), BF16), deep, deep, deep, deep,
        half, wide, vm((rows, 128), F32), wide, wide, half,
        half, vm((K, E, H), BF16), vm((K, E, H), BF16), vm((K, E, H), BF16),
        half, vm((rows, rows), BF16), vm((3, 2, DP, S, hs, E), BF16), vm((3, 2, 2, S, hs, E), BF16), owned, owned,
        vm((3, 2, 4, hs, E), BF16), vm((3, 2, 4, hs, E), BF16), fourth, fourth, vm((2, 2, 4, hs, E), BF16), vm((2, 2, 4, hs, E), BF16), vm((3, 2, 4, hs, E), BF16), vm((3, 2, 4, hs, E), BF16), vm((3, 2, 2, hs, E), BF16), vm((3, 2, 2, hs, E), BF16),
        vm((3, 2, hs, E), BF16), vm((3, 2, hs, E), BF16),
        vm((2, DP, share + 16, rows // 2), BF16), vm((2, DP, share + 16, rows // 2), BF16),
        dma((4, 2, S)), dma((4, 2, S)), dma((3, 2, 2)), dma((3, 2, 2)), dma((3, 2)), dma((3, 2)),
        dma((3, 2)), dma((3, 2)), dma((3, 2)), dma((3, 2)), dma((3, 2)), dma((3, 2)), dma((2, DP)), dma((2, DP)), dma((3, 2, 4)), dma((3, 2, 4)), dma((4,)),
    ]
    whole = pl.BlockSpec(memory_space=pltpu.VMEM)
    away = pl.BlockSpec(memory_space=pl.ANY)
    gtok, facs, wout = pl.pallas_call(
        lambda *refs: fused(S, DP, *refs),
        out_shape=(
            jax.ShapeDtypeStruct(full, BF16),
            jax.ShapeDtypeStruct((share + 16, rows), F32),
            jax.ShapeDtypeStruct((3, kd * hs, E), F32),
        ),
        in_specs=[whole, away] + [whole] * 6 + [away] * 3,
        out_specs=(whole,) * 3,
        scratch_shapes=scratch,
        compiler_params=pltpu.CompilerParams(
            collective_id=0, has_side_effects=True, vmem_limit_bytes=62 * 1024 * 1024
        ),
    )(tokens[0], cotangent[0], first_factor[0], split, *gains, gate_weight, up_weight, down_weight)
    outs = pl.pallas_call(
        lambda *refs: arrange(S, share, part, kd, hs // K, *refs),
        out_shape=(
            jax.ShapeDtypeStruct(full, BF16),
            jax.ShapeDtypeStruct((share, rows), F32),
            jax.ShapeDtypeStruct((S, nbd, ic), F32),
            jax.ShapeDtypeStruct((kd * hs, E), F32),
            jax.ShapeDtypeStruct((kd * hs, E), F32),
            jax.ShapeDtypeStruct((kd * hs, E), F32),
        ),
        in_specs=[whole] * 3,
        out_specs=(whole,) * 6,
    )(gtok, facs, wout)
    gtok, first, second, gate, up, down = outs
    gate, up, down = [jnp.transpose(w.reshape(kd, hs, E), (0, 2, 1)) for w in (gate, up, down)]
    return gtok[None], first.T[None], jnp.transpose(second, (0, 2, 1)), gate, up, down


def body(*args):
    S, DP = lax.axis_size("seq"), lax.axis_size("dp")
    blocks, rows = args[2].shape[:2]
    K, E, H = args[8].shape
    fits = (
        S == 8 and blocks == 1 and args[0].shape[0] == 1 and args[0].shape[1] == rows and rows == S * 2 * ROWS
        and DP == 4 and S % DP == 0 and S // DP <= 16 and S <= 128
        and E == 128 and H == K * 64 and K == 2 * DP and 64 % (8 * S) == 0
    )
    return fused_body(*args) if fits else plain_body(*args)


def solution(mesh):
    placed = (
        P("dp", "seq", None),
        P("dp", "seq", None),
        P("seq", None, None),
        P(None, "seq", None),
        P(),
        P(),
        P(),
        P(),
        P(),
        P(),
        P(),
    )
    return jax.shard_map(
        body,
        mesh=mesh,
        in_specs=placed,
        out_specs=(
            P("dp", "seq", None),
            P("seq", None, "dp"),
            P(None, "seq", "dp"),
            P("dp", None, "seq"),
            P("dp", None, "seq"),
            P("dp", None, "seq"),
        ),
        check_vma=False,
    )
```

```python
import jax
import jax.numpy as jnp
from jax import lax
from jax.experimental import pallas as pl
from jax.experimental.pallas import tpu as pltpu
from jax.sharding import PartitionSpec as P

epsilon = 1e-05


def inverse_rms(values):
    return lax.rsqrt(jnp.mean(values * values, axis=-1, keepdims=True) + epsilon)


def norm_backward(grad_normed, normed_values, inverse):
    return inverse * (
        grad_normed - normed_values * jnp.mean(grad_normed * normed_values, axis=-1, keepdims=True)
    )


def plain_body(
    tokens,
    cotangent,
    first_factor,
    second_factor,
    norm_gain,
    gate_scale,
    gate_bias,
    mlp_gain,
    gate_weight,
    up_weight,
    down_weight,
):
    inputs = tokens[0]
    upstream = cotangent[0]
    rows_local, width = inputs.shape
    local_blocks, block_size = (first_factor.shape[0], first_factor.shape[1])
    mlp_blocks, block_in, block_hidden = gate_weight.shape
    inputs_wide = inputs.astype(jnp.float32)
    first_inverse = inverse_rms(inputs_wide)
    first_normed = inputs_wide * first_inverse
    normed_tokens = (first_normed * norm_gain).astype(jnp.bfloat16)
    blocked = normed_tokens.reshape(local_blocks, block_size, width)
    section_one = jnp.einsum(
        "bij,bjd->bid", first_factor, blocked, preferred_element_type=jnp.float32
    ).astype(jnp.bfloat16)
    section_cols = lax.all_to_all(section_one, "seq", split_axis=1, concat_axis=0, tiled=True)
    mixed_cols = jnp.einsum(
        "cib,bid->cid", second_factor, section_cols, preferred_element_type=jnp.float32
    ).astype(jnp.bfloat16)
    mixed_rows = lax.all_to_all(mixed_cols, "seq", split_axis=0, concat_axis=1, tiled=True).reshape(
        rows_local, width
    )
    mixed_wide = mixed_rows.astype(jnp.float32)
    gate_open = jax.nn.sigmoid(normed_tokens.astype(jnp.float32) * gate_scale + gate_bias)
    after_mix = (inputs_wide + mixed_wide * gate_open).astype(jnp.bfloat16)
    after_wide = after_mix.astype(jnp.float32)
    second_inverse = inverse_rms(after_wide)
    second_normed = after_wide * second_inverse
    mlp_input = (
        (second_normed * mlp_gain).astype(jnp.bfloat16).reshape(rows_local, mlp_blocks, block_in)
    )
    pre_gate = jnp.einsum(
        "tkd,kdh->tkh", mlp_input, gate_weight, preferred_element_type=jnp.float32
    )
    pre_up = jnp.einsum("tkd,kdh->tkh", mlp_input, up_weight, preferred_element_type=jnp.float32)
    sig_gate = jax.nn.sigmoid(pre_gate)
    hidden = (pre_gate * sig_gate * pre_up).astype(jnp.bfloat16)
    permuted = jnp.transpose(hidden, (0, 2, 1)).reshape(rows_local, mlp_blocks, block_hidden)
    upstream_wide = upstream.astype(jnp.float32)
    upstream_blocks = upstream.reshape(rows_local, mlp_blocks, block_in)
    grad_perm = jnp.einsum(
        "tkd,kdh->tkh", upstream_blocks, down_weight, preferred_element_type=jnp.float32
    ).astype(jnp.bfloat16)
    grad_hidden = jnp.transpose(
        grad_perm.reshape(rows_local, block_hidden, mlp_blocks), (0, 2, 1)
    ).astype(jnp.float32)
    grad_gate_pre = (grad_hidden * pre_up * sig_gate * (1.0 + pre_gate * (1.0 - sig_gate))).astype(
        jnp.bfloat16
    )
    grad_up_pre = (grad_hidden * pre_gate * sig_gate).astype(jnp.bfloat16)
    grad_inner = jnp.einsum(
        "tkh,kdh->tkd", grad_gate_pre, gate_weight, preferred_element_type=jnp.float32
    )
    grad_inner = grad_inner + jnp.einsum(
        "tkh,kdh->tkd", grad_up_pre, up_weight, preferred_element_type=jnp.float32
    )
    grad_inner = grad_inner.reshape(rows_local, width)
    grad_after = (
        upstream_wide + norm_backward(grad_inner * mlp_gain, second_normed, second_inverse)
    ).astype(jnp.bfloat16)
    grad_after_wide = grad_after.astype(jnp.float32)
    grad_mixed = (grad_after_wide * gate_open).astype(jnp.bfloat16)
    grad_open = grad_after_wide * mixed_wide * gate_open * (1.0 - gate_open)
    grad_mixed_cols = lax.all_to_all(
        grad_mixed.reshape(local_blocks, block_size, width),
        "seq",
        split_axis=1,
        concat_axis=0,
        tiled=True,
    )
    grad_section_cols = jnp.einsum(
        "cib,cid->bid", second_factor, grad_mixed_cols, preferred_element_type=jnp.float32
    ).astype(jnp.bfloat16)
    second_term = jnp.einsum(
        "cid,bid->cib", grad_mixed_cols, section_cols, preferred_element_type=jnp.float32
    )
    grad_section = lax.all_to_all(grad_section_cols, "seq", split_axis=0, concat_axis=1, tiled=True)
    first_term = jnp.einsum(
        "bid,bjd->bij", grad_section, blocked, preferred_element_type=jnp.float32
    )
    grad_normed = jnp.einsum(
        "bij,bid->bjd", first_factor, grad_section, preferred_element_type=jnp.float32
    ).reshape(rows_local, width)
    grad_normed = grad_normed + grad_open * gate_scale
    grad_inputs = (
        grad_after_wide + norm_backward(grad_normed * norm_gain, first_normed, first_inverse)
    ).astype(jnp.bfloat16)
    factor_first, factor_second = (
        lax.psum_scatter(
            first_term.astype(jnp.bfloat16), "dp", scatter_dimension=2, tiled=True
        ).astype(jnp.float32),
        lax.psum_scatter(
            second_term.astype(jnp.bfloat16), "dp", scatter_dimension=2, tiled=True
        ).astype(jnp.float32),
    )
    replicas = lax.axis_size("dp")
    factor_weight = (replicas * width) ** (-0.5)
    mlp_weight = (replicas * rows_local * lax.axis_size("seq")) ** (-0.5)
    gate_term = jnp.einsum(
        "tkd,tkh->kdh", mlp_input, grad_gate_pre, preferred_element_type=jnp.float32
    )
    up_term = jnp.einsum("tkd,tkh->kdh", mlp_input, grad_up_pre, preferred_element_type=jnp.float32)
    down_term = jnp.einsum(
        "tkd,tkh->kdh", upstream_blocks, permuted, preferred_element_type=jnp.float32
    )
    stacked = jnp.concatenate([gate_term, up_term, down_term], axis=1)
    seq_summed = lax.psum_scatter(stacked, "seq", scatter_dimension=2, tiled=True)
    reduced = lax.psum_scatter(seq_summed, "dp", scatter_dimension=0, tiled=True)
    reduced = reduced * mlp_weight
    grad_gate = reduced[:, 0:block_in, :]
    grad_up = reduced[:, block_in : 2 * block_in, :]
    grad_down = reduced[:, 2 * block_in : 3 * block_in, :]
    return (
        grad_inputs[None],
        factor_first * factor_weight,
        factor_second * factor_weight,
        grad_gate,
        grad_up,
        grad_down,
    )


MESH = pl.DeviceIdType.MESH
F32 = jnp.float32
BF16 = jnp.bfloat16
ROWS = 16
UNR = 8


def mm(a, b, da=1, db=0):
    return lax.dot_general(a, b, (((da,), (db,)), ((), ())), preferred_element_type=F32)


def mult(v, m):
    return v if isinstance(v, int) else pl.multiple_of(v, m)


def row_loop(total, step, fn):
    def one(n, carry):
        fn(pl.ds(mult(n * step, step), step))
        return carry

    lax.fori_loop(0, total // step, one, 0, unroll=UNR)


def count_loop(total, fn):
    def one(n, carry):
        fn(n)
        return carry

    lax.fori_loop(0, total, one, 0)


def fused(
    S, DP,
    tok, cot_in, ff, sf, gain1, scale1, bias1, gain2, gw_in, uw_in, dw_in,
    gtok, facs, wout,
    normed, sec_out, sec_cols, mc_out, mixed, opened, gm_out, gm_cols, gs_out, gs,
    mix, mix_t, onehot, w2, gh, hid, gg, gu, inner, norm2, inv2s, ginner, gos, gres,
    cot, gw, uw, dw, cotp, ffp, ws, rc, xo, rx, yo, ry, xo2, rx2, yo2, ry2, zo, rz, lo, rl, ho, rh, ft, rf,
    send, recv, csend, crecv, xsend, xrecv, ysend, yrecv, losend, lorecv, hisend, hirecv, fsend, frecv, zsend, zrecv, lsem,
):
    me = lax.axis_index("seq")
    dp = lax.axis_index("dp")
    core = lax.rem(dp, 2)
    peer_core = dp + 1 - 2 * core
    peer_x = lax.rem(dp + 2, DP)
    rows, width = tok.shape
    K, E, H = gw.shape
    chunk = H // K
    ic = rows // S
    hs = H // S
    nbd = S // DP
    kd = K // DP
    half = rows // 2
    part = ic // 2
    ZS = S // 2
    yy = lax.rem(me, 2)
    lo_z = lax.rem(lax.div(me, 2), 2)
    hi_z = lax.div(me, 4)

    loads = []
    for n, (a, b) in enumerate(((cot_in, cot), (dw_in, dw), (gw_in, gw), (uw_in, uw))):
        load = pltpu.make_async_copy(a, b, lsem.at[n])
        load.start()
        loads.append(load)
    barrier = pltpu.get_barrier_semaphore()
    for r in range(1, S):
        pl.semaphore_signal(barrier, inc=1, device_id={"seq": lax.rem(me + r, S)}, device_id_type=MESH)
    for r in range(1, DP):
        pl.semaphore_signal(barrier, inc=1, device_id={"dp": lax.rem(dp + r, DP)}, device_id_type=MESH)

    def first_norm(s):
        v = tok[s, :].astype(F32)
        inv = lax.rsqrt(jnp.mean(v * v, axis=-1, keepdims=True) + epsilon)
        normed[s, :] = (v * inv * gain1[...]).astype(BF16)

    row_loop(rows, ROWS, first_norm)
    for q in range(S):
        for h in range(2):
            ffp[h * half + q * part : h * half + (q + 1) * part, :] = ff[q * ic + h * part : q * ic + (h + 1) * part, :]

    def aligned(start):
        return pl.ds(mult(start, part), part)

    def exchange(phase, h, src, dst):
        def where(ref, q):
            return ref.at[h, aligned(q * part)]

        copies = []
        for r in sorted(range(1, S), key=lambda r: abs(2 * r - S - 1)):
            q = lax.rem(me + r, S)
            cp = pltpu.make_async_remote_copy(
                src_ref=where(src, q),
                dst_ref=where(dst, me),
                send_sem=send.at[phase, h, r],
                recv_sem=recv.at[phase, h, r],
                device_id={"seq": q},
                device_id_type=MESH,
            )
            cp.start()
            copies.append(cp)
        where(dst, me)[...] = where(src, me)[...]
        return copies

    pending = []
    one = []
    for h in range(2):
        sec_out[h] = mm(ffp[h * half : (h + 1) * half, :], normed[...]).astype(BF16)
        if h == 0:
            pl.semaphore_wait(barrier, S - 1 + DP - 1)
        one.append(exchange(0, h, sec_out, sec_cols))
    pending += one[0] + one[1]

    def open_gate(s):
        opened[s, :] = jax.nn.sigmoid(normed[s, :].astype(F32) * scale1[...] + bias1[...])

    row_loop(rows, ROWS, open_gate)
    ri = lax.broadcasted_iota(jnp.int32, (half, half), 0)
    ci = lax.broadcasted_iota(jnp.int32, (half, half), 1)
    same = lax.rem(ri, part) == lax.rem(ci, part)
    er = lax.broadcasted_iota(jnp.int32, (half, S), 0)
    ec = lax.broadcasted_iota(jnp.int32, (half, S), 1)
    expand = jnp.where(lax.div(er, part) == ec, 1.0, 0.0).astype(BF16)
    pi = lax.broadcasted_iota(jnp.int32, (part, half), 0)
    pj = lax.rem(lax.broadcasted_iota(jnp.int32, (part, half), 1), part)
    for c in range(S):
        spread_c = mm(sf[c], expand, 0, 1)
        for h in range(2):
            rows_c = jnp.where(pi == pj, spread_c[h * part : (h + 1) * part, :], 0.0)
            mix[h, c * part : (c + 1) * part, :] = rows_c.astype(BF16)
    for h in range(2):
        mix_t[h] = jnp.transpose(mix[h].astype(F32)).astype(BF16)

    def regroup(n):
        for h in range(2):
            cotp[aligned(h * half + n * part), :] = cot[aligned(n * ic + h * part), :]

    loads[0].wait()
    count_loop(S, regroup)

    def hot_rows(s):
        hi = lax.broadcasted_iota(jnp.int32, (ROWS, K * 128), 0) + s.start
        hc = lax.broadcasted_iota(jnp.int32, (ROWS, K * 128), 1)
        lane = lax.rem(hc, 128)
        hit = hi == lax.rem(lane, chunk) * K + lax.div(hc, 128)
        for r in range(2):
            onehot[r, s, :] = jnp.where(hit & (lax.div(lane, chunk) == r), 1.0, 0.0).astype(BF16)

    row_loop(H, ROWS, hot_rows)

    def spread(p):
        for r in range(2):
            w2[p, r * E : (r + 1) * E, :] = mm(dw[2 * p + r], onehot[r]).astype(BF16)

    loads[1].wait()
    for p in range(K // 2):
        spread(p)
    two = []
    for h in range(2):
        for cp in one[h]:
            cp.wait_recv()
        mc_out[h] = mm(mix[h], sec_cols[h]).astype(BF16)
        two.append(exchange(1, h, mc_out, mixed))
    pending += two[0] + two[1]

    def hidden_grad(p):
        g = mm(cotp[:, pl.ds(mult(p * 2 * E, 2 * E), 2 * E)], w2[p]).astype(BF16)
        for k in range(K):
            gh[k, :, pl.ds(mult(p * 128, 128), 128)] = g[:, k * 128 : (k + 1) * 128]

    for p in range(K // 2):
        hidden_grad(p)
    def second_norm(h, n):
        nat, own = aligned(n * ic + h * part), aligned(n * part)
        s = aligned(h * half + n * part)
        resid = (tok[nat, :].astype(F32) + mixed[h, own, :].astype(F32) * opened[nat, :]).astype(BF16).astype(F32)
        inv = lax.rsqrt(jnp.mean(resid * resid, axis=-1, keepdims=True) + epsilon)
        n2 = resid * inv
        norm2[s, :] = n2
        inv2s[s, :] = jnp.broadcast_to(inv, (part, 128))
        inner[s, :] = (n2 * gain2[...]).astype(BF16)

    def mlp(h, k):
        cols = slice(k * E, k * E + E)
        mine = slice(h * half, (h + 1) * half)
        x = inner[mine, cols]
        for c0 in range(0, H, 256):
            cs = slice(c0, c0 + 256)
            va = mm(x, gw[k, :, cs])
            vu = mm(x, uw[k, :, cs])
            for n in range(0, half, 16):
                a, u = va[n : n + 16], vu[n : n + 16]
                t = slice(h * half + n, h * half + n + 16)
                g = gh[k, t, cs].astype(F32)
                sig = 0.5 * jnp.tanh(0.5 * a) + 0.5
                silu = a * sig
                hid[k, t, cs] = (silu * u).astype(BF16)
                gg[k, t, cs] = (g * u * (sig + silu * (1.0 - sig))).astype(BF16)
                gu[k, t, cs] = (g * silu).astype(BF16)
        ginner[mine, cols] = mm(gg[k, mine, :], gw[k], 1, 1) + mm(gu[k, mine, :], uw[k], 1, 1)

    def second_back(h, n):
        nat, own = aligned(n * ic + h * part), aligned(n * part)
        s = aligned(h * half + n * part)
        n2 = norm2[s, :]
        dn = ginner[s, :] * gain2[...]
        mean = jnp.mean(dn * n2, axis=-1, keepdims=True)
        gr = (cot[nat, :].astype(F32) + inv2s[s, 0:1] * (dn - n2 * mean)).astype(BF16)
        gres[nat, :] = gr
        wide = gr.astype(F32)
        op = opened[nat, :]
        gm_out[h, own, :] = (wide * op).astype(BF16)
        gos[nat, :] = wide * mixed[h, own, :].astype(F32) * op * (1.0 - op) * scale1[...]

    three = []
    share = rows // DP
    pr = lax.broadcasted_iota(jnp.int32, (DP * 16, half), 0)
    pc = lax.div(lax.broadcasted_iota(jnp.int32, (DP * 16, half), 1), part)
    pick = (lax.div(pr, 16) == lax.div(pc, nbd)) & (lax.rem(pr, 16) == lax.rem(pc, nbd))
    pick = jnp.where(pick, 1.0, 0.0).astype(BF16)
    four = [None, None]

    def back_mix(h):
        for cp in three[h]:
            cp.wait_recv()
        gs_out[h] = mm(mix_t[h], gm_cols[h]).astype(BF16)
        four[h] = exchange(3, h, gs_out, gs)
        pending.extend(four[h])

    def outer(h):
        both = jnp.where(same, mm(sec_cols[h], gm_cols[h], 1, 1), 0.0).astype(BF16)
        picked = mm(pick, both).astype(BF16)
        for d in range(DP):
            ft[h, d, share : share + 16, :] = picked[d * 16 : (d + 1) * 16, :]

    arrivals = {}
    y_units = ((0, 1),)
    z_units = ((0, 0), (0, 1), (2, 0), (2, 1))
    early = []

    def mark():
        early.extend(pending)
        pending.clear()

    def drain():
        for cp in early:
            cp.wait_send()

    def start(key, src, dst, send_sem, recv_sem, device):
        cp = pltpu.make_async_remote_copy(
            src_ref=src, dst_ref=dst, send_sem=send_sem, recv_sem=recv_sem, device_id=device, device_id_type=MESH
        )
        cp.start()
        arrivals[key] = cp
        pending.append(cp)

    far_mine = lax.rem(dp + 2, DP)
    far_peer = lax.rem(peer_core + 2, DP)

    def spot(q):
        return (q % 2) * 4 + (q // 2) % 2 * 2 + q // 4

    def down_term(p):
        c = cotp[:, 2 * p * E : 2 * (p + 1) * E]
        raws = [mm(hid[k, :, p * 128 : (p + 1) * 128], c, 0, 0) for k in range(K)]
        for r in range(2):
            parts = [raw[r * chunk : (r + 1) * chunk, r * E : (r + 1) * E] for raw in raws]
            size = chunk // S
            for q in range(S):
                piece = jnp.concatenate([v[q * size : (q + 1) * size, :] for v in parts], axis=0)
                ws[0, r, p, spot(q)] = piece.astype(BF16)

    def in_term(j, grads, p):
        for r in range(2):
            x = inner[:, (2 * p + r) * E : (2 * p + r + 1) * E]
            raw = mm(grads[2 * p + r], x, 0, 0).astype(BF16)
            for q in range(S):
                ws[j, r, p, spot(q)] = raw[q * hs : (q + 1) * hs, :]

    def to_core(j):
        for slot, owner in enumerate((far_peer, peer_core)):
            for r in range(2):
                start(
                    ("c", j, r, slot), ws.at[j, r, owner], rc.at[j, r, slot],
                    csend.at[j, r, slot], crecv.at[j, r, slot], {"dp": peer_core},
                )

    def down_terms():
        for p in range(K // 2):
            down_term(p)
        to_core(0)

    def near_sum(j, r, q, slot):
        owner = dp if slot else far_mine
        return ws[j, r, owner, q].astype(F32) + rc[j, r, slot, q].astype(F32)

    def y_first(r):
        for slot in range(2):
            arrivals["c", 0, r, slot].wait_recv()
            for z in range(4):
                yo2[r, slot, z] = near_sum(0, r, (1 - yy) * 4 + z, slot).astype(BF16)
        start(("y", 0, r), yo2.at[r], ry2.at[r], ysend.at[0, r], yrecv.at[0, r], {"seq": me + 1 - 2 * yy})

    def x_second(r):
        arrivals["y", 0, r].wait_recv()
        for z in range(4):
            xo2[r, z] = (near_sum(0, r, yy * 4 + z, 0) + ry2[r, 0, z].astype(F32)).astype(BF16)
        start(("x", 0, r), xo2.at[r], rx2.at[r], xsend.at[0, r], xrecv.at[0, r], {"dp": peer_x})

    def over_x(j, r):
        arrivals["c", j, r, 0].wait_recv()
        for q in range(S):
            xo[j, r, q] = (ws[j, r, far_mine, q].astype(F32) + rc[j, r, 0, q].astype(F32)).astype(BF16)
        start(("x", j, r), xo.at[j, r], rx.at[j, r], xsend.at[j, r], xrecv.at[j, r], {"dp": peer_x})

    def partial(j, r, q):
        return ws[j, r, dp, q].astype(F32) + rc[j, r, 1, q].astype(F32) + rx[j, r, q].astype(F32)

    def over_y(j, r):
        arrivals["c", j, r, 1].wait_recv()
        arrivals["x", j, r].wait_recv()
        for z in range(4):
            yo[j, r, z] = partial(j, r, (1 - yy) * 4 + z).astype(BF16)
        start(("y", j, r), yo.at[j, r], ry.at[j, r], ysend.at[j, r], yrecv.at[j, r], {"seq": me + 1 - 2 * yy})

    def after_y(j, r, z):
        if (j, r) in y_units:
            return near_sum(0, r, yy * 4 + z, 1) + ry2[r, 1, z].astype(F32) + rx2[r, z].astype(F32)
        return partial(j, r, yy * 4 + z) + ry[j, r, z].astype(F32)

    def over_lo(j, r):
        arrivals["x" if (j, r) in y_units else "y", j, r].wait_recv()
        for z in range(2):
            lo[j, r, z] = after_y(j, r, (1 - lo_z) * 2 + z).astype(BF16)
        start(("l", j, r), lo.at[j, r], rl.at[j, r], losend.at[j, r], lorecv.at[j, r], {"seq": me + 2 - 4 * lo_z})

    def after_lo(j, r, z):
        return after_y(j, r, lo_z * 2 + z) + rl[j, r, z].astype(F32)

    def over_hi(j, r):
        arrivals["l", j, r].wait_recv()
        ho[j, r] = after_lo(j, r, 1 - hi_z).astype(BF16)
        start(("h", j, r), ho.at[j, r], rh.at[j, r], hisend.at[j, r], hirecv.at[j, r], {"seq": me + 4 - 8 * hi_z})

    def over_z(j, r):
        arrivals["x" if (j, r) in y_units else "y", j, r].wait_recv()
        for n in range(1, 4):
            z = lax.rem(hi_z * 2 + lo_z + n, 4)
            zo[j, r, n] = after_y(j, r, lax.rem(z, 2) * 2 + lax.div(z, 2)).astype(BF16)
            start(("z", j, r, n), zo.at[j, r, n], rz.at[j, r, n], zsend.at[j, r, n], zrecv.at[j, r, n], {"seq": z * 2 + yy})

    def finish(j, r):
        scale = (DP * rows * S) ** (-0.5)
        if (j, r) in z_units:
            total = after_y(j, r, lo_z * 2 + hi_z)
            for n in range(1, 4):
                arrivals["z", j, r, n].wait_recv()
                total = total + rz[j, r, n].astype(F32)
            wout[j, r * hs : (r + 1) * hs, :] = total * scale
            return
        arrivals["h", j, r].wait_recv()
        wout[j, r * hs : (r + 1) * hs, :] = (after_lo(j, r, hi_z) + rh[j, r].astype(F32)) * scale

    def factor(h):
        for cp in four[h]:
            cp.wait_recv()
        f1 = mm(normed[...], gs[h], 1, 1).astype(BF16)
        for d in range(DP):
            ft[h, d, 0:share, :] = f1[d * share : (d + 1) * share, :]
        for r in sorted(range(1, DP), key=lambda r: abs(r - DP // 2)):
            d = lax.rem(dp + r, DP)
            start(("f", h, r), ft.at[h, d], rf.at[h, r], fsend.at[h, r], frecv.at[h, r], {"dp": d})

    def first_back(s):
        v = tok[s, :].astype(F32)
        inv = lax.rsqrt(jnp.mean(v * v, axis=-1, keepdims=True) + epsilon)
        n1 = v * inv
        dm = (ginner[s, :] + gos[s, :]) * gain1[...]
        mean = jnp.mean(dm * n1, axis=-1, keepdims=True)
        gtok[s, :] = (gres[s, :].astype(F32) + inv * (dm - n1 * mean)).astype(BF16)

    def token_grad():
        ginner[...] = mm(ffp[...], gs[...].reshape(rows, width), 0, 0)
        row_loop(rows, ROWS, first_back)

    def factor_sum(h):
        for r in range(1, DP):
            arrivals["f", h, r].wait_recv()
        total = ft[h, dp].astype(F32)
        for r in range(1, DP):
            total = total + rf[h, r].astype(F32)
        facs[:, h * half : (h + 1) * half] = total * ((DP * width) ** (-0.5))

    loads[2].wait()
    loads[3].wait()
    for h in range(2):
        for cp in two[h]:
            cp.wait_recv()
        for n in range(S):
            second_norm(h, n)
        for k in range(K):
            mlp(h, k)
            if h == 1 and k % 2 == 1:
                in_term(1, gg, k // 2)
                in_term(2, gu, k // 2)
        if h == 1:
            to_core(1)
            to_core(2)
        for n in range(S):
            second_back(h, n)
        three.append(exchange(2, h, gm_out, gm_cols))
    pending += three[0] + three[1]
    over_x(1, 0)
    over_x(1, 1)
    over_x(2, 0)
    over_x(2, 1)
    down_terms()
    mark()
    back_mix(0)
    over_x(0, 0)
    y_first(1)
    outer(0)
    back_mix(1)
    outer(1)
    over_y(1, 0)
    over_y(1, 1)
    over_y(2, 0)
    x_second(1)
    over_y(2, 1)
    over_lo(1, 0)
    over_lo(1, 1)
    factor(0)
    over_z(2, 0)
    drain()
    factor(1)
    over_z(2, 1)
    over_hi(1, 0)
    over_hi(1, 1)
    over_y(0, 0)
    over_z(0, 1)
    token_grad()
    over_z(0, 0)
    finish(1, 0)
    finish(1, 1)
    finish(2, 0)
    factor_sum(0)
    finish(2, 1)
    factor_sum(1)
    finish(0, 1)
    finish(0, 0)
    for cp in pending:
        cp.wait_send()


def arrange(S, share, part, kd, step, gtok_in, facs, wout, gtok, first, second, gate, up, down):
    gtok[...] = gtok_in[...]
    nbd = second.shape[1]
    half = S * part
    pieces = [facs[0:share, h * half + q * part : h * half + (q + 1) * part] for q in range(S) for h in range(2)]
    first[...] = jnp.concatenate(pieces, axis=1)
    for c in range(S):
        pieces = [facs[share : share + nbd, h * half + c * part : h * half + (c + 1) * part] for h in range(2)]
        second[c] = jnp.concatenate(pieces, axis=1)
    gate[...] = wout[1]
    up[...] = wout[2]
    size = wout.shape[1] // kd
    K = size // step
    for d in range(kd):
        for k in range(K):
            at = d * size + k * step
            down[pl.ds(d * size + k, step, stride=K), :] = wout[0, at : at + step, :]


def fused_body(
    tokens, cotangent, first_factor, second_factor, norm_gain, gate_scale, gate_bias, mlp_gain,
    gate_weight, up_weight, down_weight,
):
    S, DP = lax.axis_size("seq"), lax.axis_size("dp")
    rows, width = tokens.shape[1:]
    K, E, H = gate_weight.shape
    ic = rows // S
    nbd = S // DP
    hs = H // S
    kd = K // DP
    share = rows // DP
    part = ic // 2
    split = jnp.transpose(second_factor, (0, 2, 1))
    gains = [v.reshape(1, width) for v in (norm_gain, gate_scale, gate_bias, mlp_gain)]
    full = (rows, width)
    vm = pltpu.VMEM
    fourth = vm((2, 4, hs, E), BF16)
    owned = vm((3, 2, S, hs, E), BF16)
    wide = vm(full, F32)
    half = vm(full, BF16)
    pair = vm((2, rows // 2, width), BF16)
    deep = vm((K, rows, H), BF16)
    dma = pltpu.SemaphoreType.DMA
    scratch = [
        half, pair, pair, pair, pair, wide, pair, pair, pair, pair,
        vm((2, rows // 2, rows // 2), BF16), vm((2, rows // 2, rows // 2), BF16), vm((2, H, K * 128), BF16),
        vm((K // 2, 2 * E, K * 128), BF16), deep, deep, deep, deep,
        half, wide, vm((rows, 128), F32), wide, wide, half,
        half, vm((K, E, H), BF16), vm((K, E, H), BF16), vm((K, E, H), BF16),
        half, vm((rows, rows), BF16), vm((3, 2, DP, S, hs, E), BF16), vm((3, 2, 2, S, hs, E), BF16), owned, owned,
        vm((3, 2, 4, hs, E), BF16), vm((3, 2, 4, hs, E), BF16), fourth, fourth, vm((2, 2, 4, hs, E), BF16), vm((2, 2, 4, hs, E), BF16), vm((3, 2, 4, hs, E), BF16), vm((3, 2, 4, hs, E), BF16), vm((3, 2, 2, hs, E), BF16), vm((3, 2, 2, hs, E), BF16),
        vm((3, 2, hs, E), BF16), vm((3, 2, hs, E), BF16),
        vm((2, DP, share + 16, rows // 2), BF16), vm((2, DP, share + 16, rows // 2), BF16),
        dma((4, 2, S)), dma((4, 2, S)), dma((3, 2, 2)), dma((3, 2, 2)), dma((3, 2)), dma((3, 2)),
        dma((3, 2)), dma((3, 2)), dma((3, 2)), dma((3, 2)), dma((3, 2)), dma((3, 2)), dma((2, DP)), dma((2, DP)), dma((3, 2, 4)), dma((3, 2, 4)), dma((4,)),
    ]
    whole = pl.BlockSpec(memory_space=pltpu.VMEM)
    away = pl.BlockSpec(memory_space=pl.ANY)
    gtok, facs, wout = pl.pallas_call(
        lambda *refs: fused(S, DP, *refs),
        out_shape=(
            jax.ShapeDtypeStruct(full, BF16),
            jax.ShapeDtypeStruct((share + 16, rows), F32),
            jax.ShapeDtypeStruct((3, kd * hs, E), F32),
        ),
        in_specs=[whole, away] + [whole] * 6 + [away] * 3,
        out_specs=(whole,) * 3,
        scratch_shapes=scratch,
        compiler_params=pltpu.CompilerParams(
            collective_id=0, has_side_effects=True, vmem_limit_bytes=62 * 1024 * 1024
        ),
    )(tokens[0], cotangent[0], first_factor[0], split, *gains, gate_weight, up_weight, down_weight)
    outs = pl.pallas_call(
        lambda *refs: arrange(S, share, part, kd, hs // K, *refs),
        out_shape=(
            jax.ShapeDtypeStruct(full, BF16),
            jax.ShapeDtypeStruct((share, rows), F32),
            jax.ShapeDtypeStruct((S, nbd, ic), F32),
            jax.ShapeDtypeStruct((kd * hs, E), F32),
            jax.ShapeDtypeStruct((kd * hs, E), F32),
            jax.ShapeDtypeStruct((kd * hs, E), F32),
        ),
        in_specs=[whole] * 3,
        out_specs=(whole,) * 6,
    )(gtok, facs, wout)
    gtok, first, second, gate, up, down = outs
    gate, up, down = [jnp.transpose(w.reshape(kd, hs, E), (0, 2, 1)) for w in (gate, up, down)]
    return gtok[None], first.T[None], jnp.transpose(second, (0, 2, 1)), gate, up, down


def body(*args):
    S, DP = lax.axis_size("seq"), lax.axis_size("dp")
    blocks, rows = args[2].shape[:2]
    K, E, H = args[8].shape
    fits = (
        S == 8 and blocks == 1 and args[0].shape[0] == 1 and args[0].shape[1] == rows and rows == S * 2 * ROWS
        and DP == 4 and S % DP == 0 and S // DP <= 16 and S <= 128
        and E == 128 and H == K * 64 and K == 2 * DP and 64 % (8 * S) == 0
    )
    return fused_body(*args) if fits else plain_body(*args)


def solution(mesh):
    placed = (
        P("dp", "seq", None),
        P("dp", "seq", None),
        P("seq", None, None),
        P(None, "seq", None),
        P(),
        P(),
        P(),
        P(),
        P(),
        P(),
        P(),
    )
    return jax.shard_map(
        body,
        mesh=mesh,
        in_specs=placed,
        out_specs=(
            P("dp", "seq", None),
            P("seq", None, "dp"),
            P(None, "seq", "dp"),
            P("dp", None, "seq"),
            P("dp", None, "seq"),
            P("dp", None, "seq"),
        ),
        check_vma=False,
    )
```
